512 devices in a mesh: row: 32 (over x, y_lo, core), col: 16 (over y_hi, z).
Axes of the slice: x: 4, y: 8 (y_hi: 2, y_lo: 4; y = y_hi * 4 + y_lo), z: 8, core: 2. Of those that a mesh axis runs over, the one named last changes fastest.
Arguments:
- objects: float32 [2, 2, 4096, 4096], P(None, None, 'row', 'col'), as said below
- probe_modes: float32 [4, 2, 128, 128], replicated, may hold values from -3 to 3
- intensities: float32 [32, 16, 2, 128, 128], P('row', 'col'), may hold values from 0 to 2
- positions: int32 [32, 16, 2, 2], P('row', 'col'), may hold values from 0 to 3968, as said below
- counts: int32 [32, 16], P('row', 'col'), may hold values from 0 to 2, as said below
Outputs:
- refined_object: float32 [2, 2, 4096, 4096], P(None, None, 'row', 'col')
- refined_probe: float32 [4, 2, 128, 128], replicated
The draws below stay inside these ranges and needn't reach their ends.
Inputs may be any that keep to these rules, and one draw needn't show every extreme that they name: `positions`: for the pattern slot [i, j, k], the row of its top-left pixel plus 128 / 2 lies in [i * 128, (i + 1) * 128) and the column plus 128 / 2 in [j * 256, (j + 1) * 256); every patch lies inside the object; slot 0 of the first tile starts at pixel (0, 0) and slot 0 of the last tile ends at the object's last row and column. The live slots of a tile are its first counts[i, j] slots; some tile has all 2 live and some tile has none. `objects`: every entry lies in [-1.5, 1.5].
All inputs are finite; a program needn't handle non-finite values.
Results may differ from the reference program's by a relative error of at most 0.0003.
Values sent between devices are 32-bit elements; how exact they have to be, the bound alone decides.
No kernel may reach another device: no remote copies, remote signals or barrier semaphores. Data moves between devices by JAX's collectives and lax.ppermute only.
A program may use at most 64 MiB of HBM per device.

```python
import math
import jax
import jax.numpy as jnp
from jax import lax

TILE_R = 128
TILE_C = 256
PROBE = 128
MODES = 4
SLICES = 2
ITERS = 2
PAT_DEV = 2
OBJ_R = 4096
OBJ_C = 4096
N_ROW = 32
N_COL = 16


def window_count(marks, reach, axis):
    length = marks.shape[axis]
    pad_shape = [(0, 0), (0, 0)]
    pad_shape[axis] = (reach, reach)
    padded = jnp.pad(marks, pad_shape)
    running = jnp.cumsum(padded, axis=axis, dtype=jnp.int32)
    zero_shape = list(marks.shape)
    zero_shape[axis] = 1
    running = jnp.concatenate([jnp.zeros(zero_shape, jnp.int32), running], axis=axis)
    upper = lax_slice(running, 2 * reach + 1, length, axis)
    lower = lax_slice(running, 0, length, axis)
    return upper - lower


def lax_slice(array, start, length, axis):
    if axis == 0:
        return array[start:start + length, :]
    return array[:, start:start + length]


def draw_objects(key, part):
    base = jax.random.uniform(key, (SLICES, 2, OBJ_R, OBJ_C), jnp.float32)
    lower = jnp.array([0.6, -0.4], jnp.float32)
    spread = jnp.array([0.8, 0.8], jnp.float32)
    dark = 0.5
    corners = draw_positions(key, part).reshape(-1, 2)
    margin = PROBE // 2
    reach = max(PROBE // 8, 1)
    center_rows = corners[:, 0] + margin
    center_cols = corners[:, 1] + margin
    marks = jnp.zeros((OBJ_R, OBJ_C), jnp.int32).at[center_rows, center_cols].add(1)
    boxed = window_count(window_count(marks, reach, 0), reach, 1)
    factor = jnp.where(boxed > 0, dark, 1.0).astype(jnp.float32)
    field = lower[None, :, None, None] + spread[None, :, None, None] * base
    return field * factor[None, None, :, :]


def draw_counts(key, part):
    row_tiles = OBJ_R // TILE_R
    col_tiles = OBJ_C // TILE_C
    tiles = row_tiles * col_tiles
    first_key = jax.random.fold_in(key, 11)
    second_key = jax.random.fold_in(key, 12)
    values = jax.random.randint(first_key, (tiles,), 0, PAT_DEV + 1)
    chosen = jax.random.randint(second_key, (), 0, tiles)
    empty_tile = (chosen + 1) % tiles
    tile_ids = jnp.arange(tiles)
    values = jnp.where(tile_ids == chosen, PAT_DEV, values)
    values = jnp.where(tile_ids == empty_tile, 0, values)
    return values.reshape(row_tiles, col_tiles).astype(jnp.int32)


def draw_positions(key, part):
    row_tiles = OBJ_R // TILE_R
    col_tiles = OBJ_C // TILE_C
    margin = PROBE // 2
    row_start = jnp.arange(row_tiles, dtype=jnp.int32) * TILE_R
    col_start = jnp.arange(col_tiles, dtype=jnp.int32) * TILE_C
    row_lower = jnp.maximum(row_start, margin)
    row_upper = jnp.minimum(row_start + TILE_R, OBJ_R - margin + 1)
    col_lower = jnp.maximum(col_start, margin)
    col_upper = jnp.minimum(col_start + TILE_C, OBJ_C - margin + 1)
    shape = (row_tiles, col_tiles, PAT_DEV)
    row_centers = jax.random.randint(jax.random.fold_in(key, 21), shape, row_lower[:, None, None], row_upper[:, None, None])
    col_centers = jax.random.randint(jax.random.fold_in(key, 22), shape, col_lower[None, :, None], col_upper[None, :, None])
    row_ids = jnp.arange(row_tiles, dtype=jnp.int32)[:, None, None]
    col_ids = jnp.arange(col_tiles, dtype=jnp.int32)[None, :, None]
    slot_ids = jnp.arange(PAT_DEV, dtype=jnp.int32)[None, None, :]
    first_slot = (row_ids == 0) & (col_ids == 0) & (slot_ids == 0)
    last_slot = (row_ids == row_tiles - 1) & (col_ids == col_tiles - 1) & (slot_ids == 0)
    row_centers = jnp.where(first_slot, margin, row_centers)
    col_centers = jnp.where(first_slot, margin, col_centers)
    row_centers = jnp.where(last_slot, OBJ_R - margin, row_centers)
    col_centers = jnp.where(last_slot, OBJ_C - margin, col_centers)
    return jnp.stack([row_centers - margin, col_centers - margin], axis=-1).astype(jnp.int32)


def level_of(own_key, shape, cuts, smallest, top_value):
    loudness, own = 1.0, jax.random.fold_in(own_key, 6)
    for position, blocks in cuts:
        draws = jnp.exp(jax.random.uniform(jax.random.fold_in(own, position), (blocks,), jnp.float32, smallest / len(cuts), top_value / len(cuts)))
        loudness = loudness * jnp.repeat(draws, shape[position] // blocks).reshape([-1 if axis == position else 1 for axis in range(len(shape))])
    return loudness


def centred(stream_key, extent, scale, limit, held_as=jnp.bfloat16):
    result = scale * jax.random.normal(stream_key, extent, jnp.float32)
    return jnp.clip(result, min=-limit, max=limit).astype(held_as)


def setup_inputs(seed: int = 0) -> dict:
    streams_of = jax.random.split(jax.random.key(seed), 6)
    objects = draw_objects(jax.random.fold_in(streams_of[5], 71), 0)
    probe_modes = centred(streams_of[1], (MODES, 2, PROBE, PROBE), 0.5, 3.0, jnp.float32)
    intensities = jnp.clip(2.0 * jax.random.uniform(streams_of[2], (N_ROW, N_COL, PAT_DEV, PROBE, PROBE), jnp.float32) ** level_of(streams_of[2], (N_ROW, N_COL, PAT_DEV, PROBE, PROBE), ((0, 32), (1, 16)), -0.2, 0.2), 0.0, 2.0)
    positions = draw_positions(jax.random.fold_in(streams_of[5], 71), 0)
    counts = draw_counts(jax.random.fold_in(streams_of[5], 71), 0)
    return dict(objects=objects, probe_modes=probe_modes, intensities=intensities, positions=positions, counts=counts)


highest = lax.Precision.HIGHEST

def block_table(upper_left, upper_right, lower_left, lower_right):
    return jnp.stack([jnp.stack([upper_left, upper_right]), jnp.stack([lower_left, lower_right])])

def fourier_tables(width):
    index = jnp.arange(width, dtype=jnp.int32)
    product = index[:, None] * index[None, :] % width
    angle = product.astype(jnp.float32) * (-2.0 * math.pi / width)
    scale = 1.0 / math.sqrt(width)
    middle = width // 2
    frequency = ((index + middle) % width - middle).astype(jnp.float32)
    phase = (frequency[:, None] ** 2 + frequency[None, :] ** 2) * (-4.0 * math.pi / (width * width))
    cosine = jnp.cos(angle) * scale
    sine = jnp.sin(angle) * scale
    forward_left = block_table(cosine, -sine, sine, cosine)
    forward_right = block_table(cosine, sine, -sine, cosine)
    inverse_left = block_table(cosine, sine, -sine, cosine)
    inverse_right = block_table(cosine, -sine, sine, cosine)
    return (forward_left, forward_right, inverse_left, inverse_right, jnp.cos(phase), jnp.sin(phase))

def fourier_field(field, tables, direction):
    if direction > 0:
        left_table, right_table = (tables[0], tables[1])
    else:
        left_table, right_table = (tables[2], tables[3])
    upper = jnp.einsum('pqab,kmqbc->kmpac', left_table, field, precision=highest)
    return jnp.einsum('kmqab,qpbc->kmpac', upper, right_table, precision=highest)

def complex_product(first, second):
    real_part = first[:, :, 0] * second[:, :, 0] - first[:, :, 1] * second[:, :, 1]
    imag_part = first[:, :, 0] * second[:, :, 1] + first[:, :, 1] * second[:, :, 0]
    return jnp.stack([real_part, imag_part], axis=2)

def conj_product(first, second):
    real_part = first[:, :, 0] * second[:, :, 0] + first[:, :, 1] * second[:, :, 1]
    imag_part = first[:, :, 0] * second[:, :, 1] - first[:, :, 1] * second[:, :, 0]
    return jnp.stack([real_part, imag_part], axis=2)

def propagate(field, tables, direction):
    spectrum = fourier_field(field, tables, 1.0)
    kernel = jnp.stack([tables[4], tables[5] * direction])[None, None]
    return fourier_field(complex_product(spectrum, kernel), tables, -1.0)

def pattern_terms(probe_modes, patches, measured, live_mask, tables):
    slot_count = patches.shape[0]
    layers = patches.shape[1]
    wave = jnp.broadcast_to(probe_modes[None], (slot_count,) + probe_modes.shape)
    inputs = []
    for layer_index in range(layers):
        obj = patches[:, layer_index][:, None]
        inputs.append(wave)
        exit_wave = complex_product(wave, obj)
        if layer_index < layers - 1:
            wave = propagate(exit_wave, tables, 1.0)
        else:
            far = fourier_field(exit_wave, tables, 1.0)
    intensity = lax.optimization_barrier(jnp.sum(far * far, axis=(1, 2)))
    weight = (2.0 * (intensity - measured))[:, None, None]
    grad = fourier_field(weight * far, tables, -1.0)
    slice_grads = [None] * layers
    for layer_index in reversed(range(layers)):
        obj = patches[:, layer_index][:, None]
        slice_grads[layer_index] = lax.optimization_barrier(jnp.sum(conj_product(inputs[layer_index], grad), axis=1))
        back = conj_product(obj, grad)
        if layer_index > 0:
            grad = propagate(back, tables, -1.0)
    weights = live_mask[:, None, None, None, None]
    object_grads = jnp.stack(slice_grads, axis=1) * weights
    probe_terms = lax.optimization_barrier(jnp.sum(back * weights, axis=0))
    first = patches[:, 0]
    illumination = lax.optimization_barrier(jnp.sum(lax.optimization_barrier(jnp.sum(first * first, axis=1)) * live_mask[:, None, None], axis=0))
    return (object_grads, probe_terms, illumination)

def reference(objects, probe_modes, intensities, positions, counts):
    width = probe_modes.shape[-1]
    layers = objects.shape[0]
    tables = fourier_tables(width)
    slot_count = intensities.shape[2]
    tiles = counts.shape[0] * counts.shape[1]
    tile_corners = positions.reshape(tiles, slot_count, 2).astype(jnp.int32)
    tile_measured = intensities.reshape(tiles, slot_count, width, width)
    slot_ids = jnp.arange(slot_count, dtype=jnp.int32)
    tile_live = (slot_ids[None, :] < counts.reshape(tiles, 1)).astype(jnp.float32)
    for step_index in range(ITERS):
        current = objects
        modes_now = probe_modes

        def tile_step(carry, inputs):
            grad_field, probe_sum, light_sum = carry
            corners, measured, live_mask = inputs

            def cut_patch(corner):
                start = (jnp.int32(0), jnp.int32(0), corner[0].astype(jnp.int32), corner[1].astype(jnp.int32))
                return lax.dynamic_slice(current, start, (layers, 2, width, width))
            patches = jax.vmap(cut_patch)(corners)
            object_grads, probe_terms, illumination = pattern_terms(modes_now, patches, measured, live_mask, tables)

            def place(slot_index, field):
                corner = corners[slot_index]
                start = (jnp.int32(0), jnp.int32(0), corner[0].astype(jnp.int32), corner[1].astype(jnp.int32))
                present = lax.dynamic_slice(field, start, (layers, 2, width, width))
                return lax.dynamic_update_slice(field, present + object_grads[slot_index], start)
            grad_field = lax.fori_loop(0, slot_count, place, grad_field)
            return ((grad_field, probe_sum + probe_terms, light_sum + illumination), None)
        start_carry = (jnp.zeros(current.shape, jnp.float32), jnp.zeros(modes_now.shape, jnp.float32), jnp.zeros((width, width), jnp.float32))
        (grad_field, probe_sum, light_sum), _ = lax.scan(tile_step, start_carry, (tile_corners, tile_measured, tile_live))
        objects = current - 0.1 * grad_field
        probe_modes = modes_now - 0.25 * probe_sum / jnp.sqrt(light_sum)
    return (objects, probe_modes)
```

```python
import math

import jax
import jax.numpy as jnp
import ml_dtypes
import numpy as np
from jax import lax
from jax.experimental import pallas as pl
from jax.experimental.pallas import tpu as pltpu
from jax.sharding import Mesh, PartitionSpec as P

ROW = ("x", "yl", "c")
COL = ("yh", "z")
XZ = ("x", "z")
Y = ("yh", "yl")

W = 128
H = 64
TR = 128
TC = 256
EC = 384
M = 4
WIN = W + 8
F = 8
f32 = jnp.float32
bf16 = jnp.bfloat16


def split_np(a):
    out = []
    for _ in range(3):
        part = a.astype(ml_dtypes.bfloat16)
        out.append(part)
        a = a - part.astype(np.float64)
    return out


def tables_np():
    n = np.arange(W)
    ang = -2.0 * math.pi * ((n[:, None] * n[None, :]) % W) / W
    t = np.exp(1j * ang) / math.sqrt(W)
    f = ((n + H) % W - H).astype(np.float64)
    k = np.exp(-4j * math.pi * f * f / (W * W))
    a = np.conj(t) @ (k[:, None] * t)
    out = []
    for m in (t, a):
        u = np.block([[m.real, -m.imag], [m.imag, m.real]])
        for v in (u, u.T):
            out.extend(split_np(v))
    return np.stack(out)


def lanes(shape):
    return lax.broadcasted_iota(jnp.int32, shape, len(shape) - 1)


def split(x, parts):
    out = []
    for i in range(parts):
        h = x.astype(bf16)
        out.append(h)
        if i < parts - 1:
            x = x - h.astype(f32)
    return out


PAIRS = {2: ((0, 0), (0, 1), (1, 0)), 3: ((0, 0), (0, 1), (1, 0), (0, 2), (1, 1), (2, 0))}


def cmul(ar, ai, br, bi):
    return ar * br - ai * bi, ar * bi + ai * br


def cmulc(ar, ai, br, bi):
    return ar * br + ai * bi, ar * bi - ai * br


def right(z, lhs, tab, i, parts):
    x = jnp.concatenate([lhs[:, p * 2 * W : (p + 1) * 2 * W] for p, _ in PAIRS[parts]], axis=1)
    w = jnp.concatenate([tab[i + t] for _, t in PAIRS[parts]], axis=0)
    y = jnp.dot(x, w, preferred_element_type=f32)
    z[0] = y[:, :W].reshape(F, W, W)
    z[1] = y[:, W:].reshape(F, W, W)


def put_lhs(lhs, f, xr, xi, parts):
    rows = slice(f * W, (f + 1) * W)
    for q, x in enumerate((xr, xi)):
        for p, v in enumerate(split(x, parts)):
            at = (2 * p + q) * W
            lhs[rows, at : at + W] = v


def left(z, tab, i, f, parts):
    v = [split(jnp.concatenate([z[q, f], z[q, f + 1]], axis=1), parts) for q in range(2)]
    v = [jnp.concatenate([v[0][p], v[1][p]], axis=0) for p in range(parts)]
    x = jnp.concatenate([v[p] for p, _ in PAIRS[parts]], axis=0)
    w = jnp.concatenate([tab[i + t] for _, t in PAIRS[parts]], axis=1)
    y = jnp.dot(w, x, preferred_element_type=f32)
    return (
        (y[:W, :W], y[W:, :W]),
        (y[:W, W:], y[W:, W:]),
    )


U, UT, B, BT = 0, 3, 6, 9


def window(r0, s):
    r8 = r0 // 8
    q = s // W
    q1 = jnp.where(q == 2, 0, q + 1)
    rows = pl.ds(pl.multiple_of(r8 * 8, 8), WIN)
    at = [(rows, pl.ds(pl.multiple_of(t * W, W), W)) for t in (q, q1)]
    return at, r0 - r8 * 8, s - q * W


def cut(e, r0, s, plane):
    at, dr, dc = window(r0, s)
    low = lanes((WIN, W)) >= dc
    v = jnp.where(low, e[(plane,) + at[0]], e[(plane,) + at[1]])
    v = pltpu.roll(v, jnp.where(dc == 0, 0, W - dc), 1)
    v = pltpu.roll(v, jnp.where(dr == 0, 0, WIN - dr), 0)
    return v[:W]


def place(g, r0, s, plane, val):
    at, dr, dc = window(r0, s)
    v = jnp.concatenate([val, jnp.zeros((WIN - W, W), f32)], axis=0)
    v = pltpu.roll(v, dr, 0)
    v = pltpu.roll(v, dc, 1)
    low = lanes((WIN, W)) >= dc
    i0 = (plane,) + at[0]
    i1 = (plane,) + at[1]
    g[i0] = g[i0] + jnp.where(low, v, 0.0)
    g[i1] = g[i1] + jnp.where(low, 0.0, v)


def iteration(info, e, p, meas, tab, g, acc, z, lhs, o, psi1, parts):
    origin, positions, counts = info
    rows = [jnp.clip(positions[0, 0, n, 0] - origin[0] + H, 0, TR - 1) for n in range(2)]
    cols = [jnp.clip(positions[0, 0, n, 1] - origin[1] + W, H, TC + H - 1) for n in range(2)]
    live = [(counts[0, 0] > n).astype(f32) for n in range(2)]
    for n in range(2):
        for k in range(4):
            o[n, k] = cut(e, rows[n], cols[n], k)
    wsum = None
    for n in range(2):
        t = (o[n, 0] * o[n, 0] + o[n, 1] * o[n, 1]) * live[n]
        wsum = t if wsum is None else wsum + t
    acc[8] = wsum
    for n in range(2):
        for m in range(M):
            xr, xi = cmul(p[2 * m], p[2 * m + 1], o[n, 0], o[n, 1])
            put_lhs(lhs, n * M + m, xr, xi, parts)
    right(z, lhs, tab, BT, parts)
    for f in range(0, F, 2):
        n = f // M
        for j, (yr, yi) in enumerate(left(z, tab, B, f, parts)):
            psi1[0, f + j] = yr
            psi1[1, f + j] = yi
            xr, xi = cmul(yr, yi, o[n, 2], o[n, 3])
            put_lhs(lhs, f + j, xr, xi, parts)
    right(z, lhs, tab, UT, parts)
    for n in range(2):
        tot = None
        for f in range(n * M, (n + 1) * M, 2):
            for j, (yr, yi) in enumerate(left(z, tab, U, f, parts)):
                z[0, f + j] = yr
                z[1, f + j] = yi
                t = yr * yr + yi * yi
                tot = t if tot is None else tot + t
        wt = 2.0 * (tot - meas[n])
        for f in range(n * M, (n + 1) * M):
            put_lhs(lhs, f, wt * z[0, f], wt * z[1, f], parts)
    right(z, lhs, tab, U, parts)
    for n in range(2):
        sr = si = None
        for f in range(n * M, (n + 1) * M, 2):
            for j, (yr, yi) in enumerate(left(z, tab, UT, f, parts)):
                tr, ti = cmulc(psi1[0, f + j], psi1[1, f + j], yr, yi)
                sr = tr if sr is None else sr + tr
                si = ti if si is None else si + ti
                br, bi = cmulc(o[n, 2], o[n, 3], yr, yi)
                put_lhs(lhs, f + j, br, bi, parts)
        place(g, rows[n], cols[n], 2, sr * live[n])
        place(g, rows[n], cols[n], 3, si * live[n])
    right(z, lhs, tab, B, parts)
    for n in range(2):
        sr = si = None
        for f in range(n * M, (n + 1) * M, 2):
            for j, (yr, yi) in enumerate(left(z, tab, BT, f, parts)):
                m = f + j - n * M
                tr, ti = cmulc(p[2 * m], p[2 * m + 1], yr, yi)
                sr = tr if sr is None else sr + tr
                si = ti if si is None else si + ti
                br, bi = cmulc(o[n, 0], o[n, 1], yr, yi)
                if n == 0:
                    acc[2 * m] = br * live[n]
                    acc[2 * m + 1] = bi * live[n]
                else:
                    acc[2 * m] = acc[2 * m] + br * live[n]
                    acc[2 * m + 1] = acc[2 * m + 1] + bi * live[n]
        place(g, rows[n], cols[n], 0, sr * live[n])
        place(g, rows[n], cols[n], 1, si * live[n])


def first_kernel(origin, positions, counts, c, top, bot, p, meas, tab, e, gup, gdn, acc, g, z, lhs, o, psi1):
    e[:, 0:H, :] = top[...]
    e[:, H : H + TR, :] = c[...]
    e[:, H + TR :, :] = bot[...]
    g[...] = jnp.zeros_like(g)
    iteration((origin, positions, counts), e, p, meas, tab, g, acc, z, lhs, o, psi1, 3)
    gup[...] = g[:, 0:TR, :]
    gdn[...] = g[:, TR:, :]


def new_modes(p, s, out):
    inv = 0.25 / jnp.sqrt(s[8])
    for k in range(8):
        out[k] = p[k] - s[k] * inv


def second_kernel(origin, positions, counts, e0, r, rl, rr, p0, s, meas, tab, oc, gc, gu, gd, acc, p, g, e, z, lhs, o, psi1):
    low = lanes((256, W)) < H
    for k in range(4):
        a = rl[k]
        b = rr[k]
        e[k, :, 0:W] = e0[k, :, 0:W] - 0.1 * (r[k, :, 0:W] + jnp.where(low, b, a))
        e[k, :, W : 2 * W] = e0[k, :, W : 2 * W] - 0.1 * (r[k, :, W : 2 * W] + jnp.where(low, a, 0.0))
        e[k, :, 2 * W :] = e0[k, :, 2 * W :] - 0.1 * (r[k, :, 2 * W :] + jnp.where(low, 0.0, b))
    new_modes(p0, s, p)
    g[...] = jnp.zeros_like(g)
    iteration((origin, positions, counts), e, p, meas, tab, g, acc, z, lhs, o, psi1, 2)
    oc[...] = e[:, H : H + TR, W:]
    gc[...] = g[:, H : H + TR, :]
    gu[...] = g[:, 0:H, :]
    gd[...] = g[:, H + TR :, :]


def pack(a, b, hi):
    low = lanes(a.shape) < H
    if hi:
        return jnp.where(low, pltpu.roll(a, H, 1), b)
    return jnp.where(low, a, pltpu.roll(b, H, 1))


def strips_kernel(x, ml, mr):
    for k in range(2):
        ml[k] = pack(x[k, 0, :, 0:W], x[k, 1, :, 0:W], False)
        mr[k] = pack(x[k, 0, :, W:], x[k, 1, :, W:], True)


def widen_kernel(x, rl, rr, c, top, bot):
    low = lanes((TR, W)) < H
    for k in range(2):
        a = rl[k]
        b = rr[k]
        c[2 * k, :, 0:W] = jnp.where(low, b, pltpu.roll(a, H, 1))
        c[2 * k + 1, :, 0:W] = jnp.where(low, pltpu.roll(b, H, 1), a)
        for j in range(2):
            c[2 * k + j, :, W:] = x[k, j]
    top[...] = c[:, 0:H, :]
    bot[...] = c[:, H:, :]


def halves_kernel(gup, gdn, above, below, r, ml, mr):
    low = lanes((TR, W)) < H
    for h, (a, b) in enumerate(((gup, above), (gdn, below))):
        rows = slice(h * TR, (h + 1) * TR)
        for k in range(4):
            v = [a[k, :, j * W : (j + 1) * W] + b[k, :, j * W : (j + 1) * W] for j in range(3)]
            for j in range(3):
                r[k, rows, j * W : (j + 1) * W] = v[j]
            ml[k, rows, :] = jnp.where(low, v[1], v[0])
            mr[k, rows, :] = jnp.where(low, v[0], v[2])


def fold_kernel(gc, above, below, t, ml, mr):
    for half, b in enumerate((above, below)):
        rows = slice(half * H, (half + 1) * H)
        for k in range(2):
            v0 = gc[2 * k, rows, 0:W] + b[2 * k, :, 0:W]
            v1 = gc[2 * k + 1, rows, 0:W] + b[2 * k + 1, :, 0:W]
            ml[k, rows, :] = pack(v0, v1, True)
            mr[k, rows, :] = pack(v0, v1, False)
            for j in range(2):
                t[2 * k + j, rows, :] = gc[2 * k + j, rows, W:] + b[2 * k + j, :, W:]


def last_kernel(oc, t, rl, rr, out):
    low = lanes((TR, W)) < H
    for k in range(2):
        a = rl[k]
        b = rr[k]
        add = (
            (jnp.where(low, a, 0.0), jnp.where(low, 0.0, pltpu.roll(b, H, 1))),
            (jnp.where(low, pltpu.roll(a, H, 1), 0.0), jnp.where(low, 0.0, b)),
        )
        for j in range(2):
            for h in range(2):
                cs = slice(h * W, (h + 1) * W)
                out[k, j, :, cs] = oc[2 * k + j, :, cs] - 0.1 * (t[2 * k + j, :, cs] + add[j][h])


VM = pl.BlockSpec(memory_space=pltpu.VMEM)
SM = pl.BlockSpec(memory_space=pltpu.SMEM)


def sds(*shape):
    return jax.ShapeDtypeStruct(shape, f32)


def call(kernel, outs, *args, smem=0, scratch=(), cost=None, limit=8):
    specs = [VM] * len(args)
    for i in range(smem):
        specs[i] = SM
    return pl.pallas_call(
        kernel,
        out_shape=outs,
        in_specs=specs,
        out_specs=[VM] * len(outs) if isinstance(outs, (list, tuple)) else VM,
        scratch_shapes=list(scratch),
        compiler_params=pltpu.CompilerParams(vmem_limit_bytes=limit * 1024 * 1024),
        cost_estimate=cost,
    )(*args)


def shift(value, axes, size, step):
    if step > 0:
        perm = [(i, i + 1) for i in range(size - 1)]
    else:
        perm = [(i + 1, i) for i in range(size - 1)]
    return lax.ppermute(value, axes, perm)


def scatter_sum(v, axes, n):
    v = lax.all_to_all(v.reshape(n, 1, -1), axes, 0, 0, tiled=True)
    return jnp.sum(v, axis=(0, 1))


def spread(v, axes, n):
    w = jnp.broadcast_to(v[None, None], (n, 1) + v.shape)
    return lax.all_to_all(w, axes, 0, 0, tiled=True)


ITER_COST = pl.CostEstimate(flops=10_000_000_000, bytes_accessed=8_000_000, transcendentals=0)


def body(objects, probe_modes, intensities, positions, counts):
    tab = jnp.asarray(tables_np())
    origin = jnp.stack([lax.axis_index(ROW) * TR, lax.axis_index(COL) * TC]).astype(jnp.int32)
    modes = probe_modes.reshape(8, W, W)
    measured = intensities[0, 0]
    scratch = [
        pltpu.VMEM((4, 256, EC), f32),
        pltpu.VMEM((2, F, W, W), f32),
        pltpu.VMEM((F * W, 6 * W), bf16),
        pltpu.VMEM((2, 4, W, W), f32),
        pltpu.VMEM((2, F, W, W), f32),
    ]

    ml, mr = call(strips_kernel, [sds(2, TR, W)] * 2, objects)
    right_in = shift(ml, COL, 16, -1)
    left_in = shift(mr, COL, 16, 1)
    c, top, bot = call(
        widen_kernel, [sds(4, TR, EC), sds(4, H, EC), sds(4, H, EC)], objects, left_in, right_in
    )
    below = shift(top, ROW, 32, -1)
    above = shift(bot, ROW, 32, 1)
    e, gup, gdn, acc = call(
        first_kernel,
        [sds(4, 256, EC), sds(4, TR, EC), sds(4, TR, EC), sds(9, W, W)],
        origin, positions, counts, c, above, below, modes, measured, tab,
        smem=3, scratch=scratch, cost=ITER_COST, limit=24,
    )

    below = shift(gup, ROW, 32, -1)
    above = shift(gdn, ROW, 32, 1)
    v = scatter_sum(acc.reshape(-1), "c", 2)
    v = scatter_sum(v, XZ, 32)
    r, ml, mr = call(
        halves_kernel, [sds(4, 256, EC), sds(4, 256, W), sds(4, 256, W)], gup, gdn, above, below
    )
    v, ml, mr = lax.optimization_barrier((v, ml, mr))
    right_in = shift(ml, COL, 16, -1)
    left_in = shift(mr, COL, 16, 1)
    v = jnp.sum(spread(v, Y, 8), axis=(0, 1))
    v = spread(v, XZ, 32).reshape(-1)
    total = spread(v, "c", 2).reshape(9, W, W)
    oc, gc, gu, gd, acc, modes = call(
        second_kernel,
        [sds(4, TR, TC), sds(4, TR, EC), sds(4, H, EC), sds(4, H, EC), sds(9, W, W), sds(8, W, W)],
        origin, positions, counts, e, r, left_in, right_in, modes, total, measured, tab,
        smem=3, scratch=scratch[:1] + scratch, cost=ITER_COST, limit=24,
    )

    below = shift(gu, ROW, 32, -1)
    above = shift(gd, ROW, 32, 1)
    v = scatter_sum(acc.reshape(-1), "c", 2)
    v = scatter_sum(v, XZ, 32)
    t, ml, mr = call(
        fold_kernel, [sds(4, TR, TC), sds(2, TR, W), sds(2, TR, W)], gc, above, below
    )
    v, ml, mr = lax.optimization_barrier((v, ml, mr))
    right_in = shift(ml, COL, 16, -1)
    left_in = shift(mr, COL, 16, 1)
    v = jnp.sum(spread(v, Y, 8), axis=(0, 1))
    v = spread(v, XZ, 32).reshape(-1)
    total = spread(v, "c", 2).reshape(9, W, W)
    refined = call(last_kernel, sds(2, 2, TR, TC), oc, t, left_in, right_in)
    modes = modes - 0.25 * total[:8] / jnp.sqrt(total[8])[None]
    return refined, modes.reshape(M, 2, W, W)


def solution(mesh):
    fine = Mesh(mesh.devices.reshape(4, 4, 2, 2, 8), ("x", "yl", "c", "yh", "z"))
    return jax.shard_map(
        body,
        mesh=fine,
        in_specs=(
            P(None, None, ROW, COL),
            P(),
            P(ROW, COL, None, None, None),
            P(ROW, COL, None, None),
            P(ROW, COL),
        ),
        out_specs=(P(None, None, ROW, COL), P()),
        check_vma=False,
    )
```

```python
import math

import jax
import jax.numpy as jnp
import ml_dtypes
import numpy as np
from jax import lax
from jax.experimental import pallas as pl
from jax.experimental.pallas import tpu as pltpu
from jax.sharding import Mesh, PartitionSpec as P

ROW = ("x", "yl", "c")
COL = ("yh", "z")
XZ = ("x", "z")
Y = ("yh", "yl")

W = 128
H = 64
TR = 128
TC = 256
EC = 384
M = 4
WIN = W + 8
F = 8
f32 = jnp.float32
bf16 = jnp.bfloat16


def split_np(a):
    out = []
    for _ in range(3):
        part = a.astype(ml_dtypes.bfloat16)
        out.append(part)
        a = a - part.astype(np.float64)
    return out


def tables_np():
    n = np.arange(W)
    ang = -2.0 * math.pi * ((n[:, None] * n[None, :]) % W) / W
    t = np.exp(1j * ang) / math.sqrt(W)
    f = ((n + H) % W - H).astype(np.float64)
    k = np.exp(-4j * math.pi * f * f / (W * W))
    a = np.conj(t) @ (k[:, None] * t)
    return np.stack([np.stack([np.stack(split_np(m.real)), np.stack(split_np(m.imag))], axis=1) for m in (t, a)])


def lanes(shape):
    return lax.broadcasted_iota(jnp.int32, shape, len(shape) - 1)


def split(x, parts):
    out = []
    for i in range(parts):
        h = x.astype(bf16)
        out.append(h)
        if i < parts - 1:
            x = x - h.astype(f32)
    return out


PAIRS = {2: ((0, 0), (0, 1), (1, 0)), 3: ((0, 0), (0, 1), (1, 0), (0, 2), (1, 1), (2, 0))}


def cmul(ar, ai, br, bi):
    return ar * br - ai * bi, ar * bi + ai * br


def cmulc(ar, ai, br, bi):
    return ar * br + ai * bi, ar * bi - ai * br


def right(z, lhs, tab, i, parts):
    w = jnp.concatenate([tab[i + t] for _, t in PAIRS[parts]], axis=0)
    fs = 256 // W
    for k in range(F // fs):
        rows = slice(k * 256, (k + 1) * 256)
        x = jnp.concatenate([lhs[rows, p * 2 * W : (p + 1) * 2 * W] for p, _ in PAIRS[parts]], axis=1)
        y = jnp.dot(x, w, preferred_element_type=f32)
        z[0, k * fs : (k + 1) * fs] = y[:, :W].reshape(fs, W, W)
        z[1, k * fs : (k + 1) * fs] = y[:, W:].reshape(fs, W, W)


def put_lhs(lhs, f, xr, xi, parts):
    rows = slice(f * W, (f + 1) * W)
    for q, x in enumerate((xr, xi)):
        for p, v in enumerate(split(x, parts)):
            at = (2 * p + q) * W
            lhs[rows, at : at + W] = v


def both(z, lhs, tab, i, parts):
    right(z, lhs, tab, i, parts)
    for f in range(F):
        put_lhs(lhs, f, z[0, f].T, z[1, f].T, parts)
    right(z, lhs, tab, i, parts)


U, UT, B, BT = 0, 3, 6, 9


def build_tables(tab, blocks):
    for j in range(2):
        for part in range(3):
            re = blocks[j, part, 0]
            im = blocks[j, part, 1]
            for i, (ur, ll) in enumerate(((-im, im), (im, -im))):
                k = 6 * j + 3 * i + part
                tab[k, :W, :W] = re
                tab[k, :W, W:] = ur
                tab[k, W:, :W] = ll
                tab[k, W:, W:] = re


def window(r0, s):
    r8 = r0 // 8
    q = s // W
    q1 = jnp.where(q == 2, 0, q + 1)
    rows = pl.ds(pl.multiple_of(r8 * 8, 8), WIN)
    at = [(rows, pl.ds(pl.multiple_of(t * W, W), W)) for t in (q, q1)]
    return at, r0 - r8 * 8, s - q * W


def cut(e, r0, s, plane):
    at, dr, dc = window(r0, s)
    low = lanes((WIN, W)) >= dc
    v = jnp.where(low, e[(plane,) + at[0]], e[(plane,) + at[1]])
    v = pltpu.roll(v, jnp.where(dc == 0, 0, W - dc), 1)
    v = pltpu.roll(v, jnp.where(dr == 0, 0, WIN - dr), 0)
    return v[:W]


def place(g, r0, s, plane, val):
    at, dr, dc = window(r0, s)
    v = jnp.concatenate([val, jnp.zeros((WIN - W, W), f32)], axis=0)
    v = pltpu.roll(v, dr, 0)
    v = pltpu.roll(v, dc, 1)
    low = lanes((WIN, W)) >= dc
    i0 = (plane,) + at[0]
    i1 = (plane,) + at[1]
    g[i0] = g[i0] + jnp.where(low, v, 0.0)
    g[i1] = g[i1] + jnp.where(low, 0.0, v)


def iteration(info, e, p, meas, blocks, g, acc, s, parts, waits):
    tab, z, lhs, o, psi1 = s
    where, positions, counts = info
    rows = [jnp.clip(positions[0, 0, n, 0] - where[0] + H, 0, TR - 1) for n in range(2)]
    cols = [jnp.clip(positions[0, 0, n, 1] - where[1] + W, H, TC + H - 1) for n in range(2)]
    live = [(counts[0, 0] > n).astype(f32) for n in range(2)]
    for k in range(4):
        waits[2](k)
        g[k] = jnp.zeros_like(g[k])
        for n in range(2):
            v = cut(e, rows[n], cols[n], k)
            o[n, k] = v if k < 2 else v.T
    waits[3]()
    wsum = None
    for n in range(2):
        t = (o[n, 0] * o[n, 0] + o[n, 1] * o[n, 1]) * live[n]
        wsum = t if wsum is None else wsum + t
    acc[8 * W :] = wsum
    for f in range(F):
        n, m = divmod(f, M)
        put_lhs(lhs, f, *cmul(p[2 * m], p[2 * m + 1], o[n, 0], o[n, 1]), parts)
    waits[0].wait()
    build_tables(tab, blocks)
    both(psi1, lhs, tab, BT, parts)
    for f in range(F):
        n = f // M
        put_lhs(lhs, f, *cmul(psi1[0, f], psi1[1, f], o[n, 2], o[n, 3]), parts)
    both(z, lhs, tab, UT, parts)
    for n in range(2):
        tot = None
        for f in range(n * M, (n + 1) * M):
            t = z[0, f] * z[0, f] + z[1, f] * z[1, f]
            tot = t if tot is None else tot + t
        if n == 0:
            waits[1].wait()
        wt = 2.0 * (tot - meas[n])
        for f in range(n * M, (n + 1) * M):
            put_lhs(lhs, f, wt * z[0, f], wt * z[1, f], parts)
    both(z, lhs, tab, U, parts)
    for n in range(2):
        sr = si = None
        for f in range(n * M, (n + 1) * M):
            tr, ti = cmulc(psi1[0, f], psi1[1, f], z[0, f], z[1, f])
            sr = tr if sr is None else sr + tr
            si = ti if si is None else si + ti
            put_lhs(lhs, f, *cmulc(o[n, 2], o[n, 3], z[0, f], z[1, f]), parts)
        place(g, rows[n], cols[n], 2, sr.T * live[n])
        place(g, rows[n], cols[n], 3, si.T * live[n])
    waits[4]()
    both(z, lhs, tab, B, parts)
    for n in range(2):
        sr = si = None
        for f in range(n * M, (n + 1) * M):
            m = f - n * M
            tr, ti = cmulc(p[2 * m], p[2 * m + 1], z[0, f], z[1, f])
            sr = tr if sr is None else sr + tr
            si = ti if si is None else si + ti
            for i, v in enumerate(cmulc(o[n, 0], o[n, 1], z[0, f], z[1, f])):
                at = slice((2 * m + i) * W, (2 * m + i + 1) * W)
                acc[at] = v * live[n] if n == 0 else acc[at] + v * live[n]
        place(g, rows[n], cols[n], 0, sr * live[n])
        place(g, rows[n], cols[n], 1, si * live[n])


def start(src, dst, sem):
    c = pltpu.make_async_copy(src, dst, sem)
    c.start()
    return c


def done(copies):
    for c in copies:
        c.wait()


def eight(i):
    return pl.multiple_of(i, 8)


HALF = 576


def send_sums(where, acc, keep, give, sems, i):
    mine = pl.ds(eight(where[2] * HALF), HALF)
    theirs = pl.ds(eight((1 - where[2]) * HALF), HALF)
    return [start(acc.at[mine], keep, sems.at[i]), start(acc.at[theirs], give, sems.at[i + 1])]


def col_messages(where, g, a, b, planes):
    low = lanes((256, W)) < H
    first = where[3] == 0
    for k in planes:
        v = [g[k, :, j * W : (j + 1) * W] for j in range(3)]
        ml = jnp.where(low, v[1], v[0])
        mr = jnp.where(low, v[0], v[2])
        a[k] = jnp.where(first, mr, ml)
        b[k] = jnp.where(first, ml, mr)


def first_kernel(
    where, positions, counts, x, ce, co, even, odd, p_in, meas_in, blocks_in,
    e_out, g_out, me, mo, keep, give,
    e, p, meas, blocks, g, acc, a, b, sems, *s,
):
    up = where[2] == 0
    at = eight(jnp.where(up, H + TR, 0))
    below = eight(H + TR - at)
    strips = [start(ce, a.at[0:2, 0:TR, :], sems.at[0]), start(co, b.at[0:2, 0:TR, :], sems.at[1])]
    ins = [
        [
            start(x.at[k], e.at[k, H : H + TR, W:], sems.at[2 + k]),
            start(even.at[k], e.at[k, pl.ds(at, H), :], sems.at[6 + k]),
            start(odd.at[k], e.at[k, pl.ds(below, H), :], sems.at[10 + k]),
        ]
        for k in range(4)
    ]
    modes_copy = start(p_in, p, sems.at[14])
    tables = start(blocks_in, blocks, sems.at[15])
    measured = start(meas_in, meas, sems.at[16])
    outs = []

    def plane(k):
        if k == 0:
            done(strips)
        done(ins[k])
        low = lanes((TR, W)) < H
        first = where[3] == 0
        left_in = jnp.where(first, b[k // 2, 0:TR], a[k // 2, 0:TR])
        right_in = jnp.where(first, a[k // 2, 0:TR], b[k // 2, 0:TR])
        e[k, H : H + TR, 0:W] = widened(left_in, right_in, k % 2, low)

    def whole():
        modes_copy.wait()
        outs.append(start(e, e_out, sems.at[17]))

    def ready(planes, i):
        col_messages(where, g, a, b, planes)
        ps = slice(planes[0], planes[-1] + 1)
        outs.append(start(a.at[ps], me.at[ps], sems.at[i]))
        outs.append(start(b.at[ps], mo.at[ps], sems.at[i + 1]))
        outs.append(start(g.at[ps], g_out.at[ps], sems.at[i + 2]))

    iteration(
        (where, positions, counts), e, p, meas, blocks, g, acc, s, 3,
        (tables, measured, plane, whole, lambda: ready((2, 3), 18)),
    )
    outs += send_sums(where, acc, keep, give, sems, 21)
    ready((0, 1), 23)
    done(outs)


def sum_copies(where, own, other, s, sems, i):
    mine = pl.ds(eight(where[2] * HALF), HALF)
    theirs = pl.ds(eight((1 - where[2]) * HALF), HALF)
    return [start(own, s.at[mine], sems.at[i]), start(other, s.at[theirs], sems.at[i + 1])]


def new_modes(p, s):
    inv = 0.25 / jnp.sqrt(s[8 * W :])
    for k in range(8):
        p[k] = p[k] - s[k * W : (k + 1) * W] * inv


def second_kernel(
    where, positions, counts, e_in, ge_in, go_in, even, odd, p_in, own, other, meas_in, blocks_in,
    oc, gc, give, go, keep, p_out,
    e, p, meas, blocks, g, acc, r, sums, sems, *s,
):
    at = eight(jnp.where(where[2] == 0, TR, 0))
    hi = pl.ds(at, TR)
    lo = pl.ds(eight(TR - at), TR)
    ins = [
        [
            start(e_in.at[k], e.at[k], sems.at[5 * k]),
            start(ge_in.at[k], g.at[k, hi, :], sems.at[5 * k + 1]),
            start(go_in.at[k], g.at[k, lo, :], sems.at[5 * k + 2]),
            start(even.at[k], r.at[k, hi, :], sems.at[5 * k + 3]),
            start(odd.at[k], r.at[k, lo, :], sems.at[5 * k + 4]),
        ]
        for k in range(4)
    ]
    sums_copies = [start(p_in, p, sems.at[20])] + sum_copies(where, own, other, sums, sems, 21)
    tables = start(blocks_in, blocks, sems.at[23])
    measured = start(meas_in, meas, sems.at[24])
    outs = []
    up = eight(jnp.where(where[2] == 0, H + TR, 0))
    down = eight(H + TR - up)

    def plane(k):
        done(ins[k])
        e[k] = e[k] - 0.1 * (g[k] + r[k])

    def whole():
        outs.append(start(e.at[:, H : H + TR, W:], oc, sems.at[25]))
        done(sums_copies)
        new_modes(p, sums)
        outs.append(start(p, p_out, sems.at[26]))

    def ready(planes, i):
        ps = slice(planes[0], planes[-1] + 1)
        outs.append(start(g.at[ps, pl.ds(down, H), :], go.at[ps], sems.at[i]))
        outs.append(start(g.at[ps, H : H + TR, :], gc.at[ps], sems.at[i + 1]))
        for k in planes:
            for j in range(3):
                rows = pl.ds(HALF + (3 * k + j) * H, H)
                outs.append(start(g.at[k, pl.ds(up, H), j * W : (j + 1) * W], give.at[rows], sems.at[30 + 3 * k + j]))

    iteration(
        (where, positions, counts), e, p, meas, blocks, g, acc, s, 2,
        (tables, measured, plane, whole, lambda: ready((2, 3), 27)),
    )
    outs += send_sums(where, acc, keep, give.at[pl.ds(0, HALF)], sems, 42)
    ready((0, 1), 44)
    done(outs)


def widened(left_in, right_in, part, low):
    if part == 0:
        return jnp.where(low, right_in, pltpu.roll(left_in, H, 1))
    return jnp.where(low, pltpu.roll(right_in, H, 1), left_in)


def pack(a, b, hi):
    low = lanes(a.shape) < H
    if hi:
        return jnp.where(low, pltpu.roll(a, H, 1), b)
    return jnp.where(low, a, pltpu.roll(b, H, 1))


def strips_kernel(where, x, even, odd):
    first = where[3] == 0
    for k in range(2):
        ml = pack(x[k, 0, :, 0:W], x[k, 1, :, 0:W], False)
        mr = pack(x[k, 0, :, W:], x[k, 1, :, W:], True)
        even[k] = jnp.where(first, mr, ml)
        odd[k] = jnp.where(first, ml, mr)


def widen_kernel(where, x, even, odd, be, bo):
    low = lanes((H, W)) < H
    first = where[3] == 0
    at = eight(jnp.where(where[2] == 0, H, 0))
    for out, rows in ((be, pl.ds(at, H)), (bo, pl.ds(eight(H - at), H))):
        for k in range(2):
            left_in = jnp.where(first, odd[k, rows], even[k, rows])
            right_in = jnp.where(first, even[k, rows], odd[k, rows])
            for j in range(2):
                out[2 * k + j, :, 0:W] = widened(left_in, right_in, j, low)
                out[2 * k + j, :, W:] = x[k, j, rows]


def halves_kernel(where, g_in, even, odd, ge, go, g, a, b, sems):
    ins = [
        [
            start(g_in.at[k], g.at[k], sems.at[3 * k]),
            start(even.at[k], a.at[k], sems.at[3 * k + 1]),
            start(odd.at[k], b.at[k], sems.at[3 * k + 2]),
        ]
        for k in range(4)
    ]
    low = lanes((256, W)) < H
    first = where[3] == 0
    at = eight(jnp.where(where[2] == 0, TR, 0))
    outs = []
    for k in range(4):
        done(ins[k])
        rl = jnp.where(first, b[k], a[k])
        rr = jnp.where(first, a[k], b[k])
        g[k, :, 0:W] = g[k, :, 0:W] + jnp.where(low, rr, rl)
        g[k, :, W : 2 * W] = g[k, :, W : 2 * W] + jnp.where(low, rl, 0.0)
        g[k, :, 2 * W :] = g[k, :, 2 * W :] + jnp.where(low, 0.0, rr)
        outs.append(start(g.at[k, pl.ds(at, TR), :], ge.at[k], sems.at[12 + 2 * k]))
        outs.append(start(g.at[k, pl.ds(eight(TR - at), TR), :], go.at[k], sems.at[13 + 2 * k]))
    done(outs)


def fold_kernel(where, oc, gc, even, odd, t, me, mo, r):
    at = eight(jnp.where(where[2] == 0, H, 0))
    for k in range(4):
        for j in range(3):
            r[k, pl.ds(at, H), j * W : (j + 1) * W] = even[HALF + (3 * k + j) * H : HALF + (3 * k + j + 1) * H]
    r[:, pl.ds(eight(H - at), H), :] = odd[...]
    first = where[3] == 0
    for k in range(4):
        t[k] = oc[k] - 0.1 * (gc[k, :, W:] + r[k, :, W:])
    for k in range(2):
        v0 = gc[2 * k, :, 0:W] + r[2 * k, :, 0:W]
        v1 = gc[2 * k + 1, :, 0:W] + r[2 * k + 1, :, 0:W]
        ml = pack(v0, v1, True)
        mr = pack(v0, v1, False)
        me[k] = jnp.where(first, mr, ml)
        mo[k] = jnp.where(first, ml, mr)


def last_kernel(where, t, even, odd, out):
    low = lanes((TR, W)) < H
    first = where[3] == 0
    for k in range(2):
        rl = jnp.where(first, odd[k], even[k])
        rr = jnp.where(first, even[k], odd[k])
        add = (
            (jnp.where(low, rl, 0.0), jnp.where(low, 0.0, pltpu.roll(rr, H, 1))),
            (jnp.where(low, pltpu.roll(rl, H, 1), 0.0), jnp.where(low, 0.0, rr)),
        )
        for j in range(2):
            for h in range(2):
                cs = slice(h * W, (h + 1) * W)
                out[k, j, :, cs] = t[2 * k + j, :, cs] - 0.1 * add[j][h]


def modes_kernel(where, p, own, other, out, s):
    s[pl.ds(eight(where[2] * HALF), HALF)] = own[...]
    s[pl.ds(eight((1 - where[2]) * HALF), HALF)] = other[...]
    out[...] = p[...]
    new_modes(out, s)


HB = pl.BlockSpec(memory_space=pltpu.HBM)
VM = pl.BlockSpec(memory_space=pltpu.VMEM)
SM = pl.BlockSpec(memory_space=pltpu.SMEM)


def sds(*shape):
    return jax.ShapeDtypeStruct(shape, f32)


def vm(*shape):
    return pltpu.VMEM(shape, f32)


def sem(n):
    return pltpu.SemaphoreType.DMA((n,))


def call(kernel, outs, smem, args, scratch=(), cost=None, big=False):
    spec = HB if big else VM
    return pl.pallas_call(
        kernel,
        out_shape=outs,
        in_specs=[SM] * len(smem) + [spec] * len(args),
        out_specs=[spec] * len(outs),
        scratch_shapes=list(scratch),
        compiler_params=pltpu.CompilerParams(vmem_limit_bytes=(63 if big else 12) * 1024 * 1024),
        cost_estimate=cost,
    )(*smem, *args)


def odd_swap(odd, axes, size):
    return lax.ppermute(odd, axes, [(i, ((i + 1) ^ 1) - 1) for i in range(1, size - 1)])


def swap(even, odd, axes, size):
    return lax.ppermute(even, axes, [(i, i ^ 1) for i in range(size)]), odd_swap(odd, axes, size)


def other_core(v):
    return lax.ppermute(v, "c", [(0, 1), (1, 0)])


def scatter_sum(v, axes, n):
    v = lax.all_to_all(v.reshape(n, 1, -1), axes, 0, 0, tiled=True)
    return jnp.sum(v, axis=(0, 1))


def spread(v, axes, n):
    w = jnp.broadcast_to(v[None, None], (n, 1) + v.shape)
    return lax.all_to_all(w, axes, 0, 0, tiled=True)


def apart(yes, f, shape):
    return lax.cond(yes, f, lambda: jnp.zeros(shape, f32))


def reduce_out(yes, keep, got):
    def step():
        v = scatter_sum(keep + got[:HALF], XZ, 32)
        return jnp.sum(spread(v, Y, 8), axis=(0, 1))

    return apart(yes, step, (2304,))


def gather_back(yes, v):
    return apart(yes, lambda: spread(v, XZ, 32).reshape(HALF, W), (HALF, W))


ITER_COST = pl.CostEstimate(flops=10_000_000_000, bytes_accessed=8_000_000, transcendentals=0)


def body(objects, probe_modes, intensities, positions, counts):
    blocks = jnp.asarray(tables_np())
    where = jnp.stack([
        lax.axis_index(ROW) * TR,
        lax.axis_index(COL) * TC,
        lax.axis_index("c"),
        lax.axis_index("z") % 2,
    ]).astype(jnp.int32)
    modes = probe_modes.reshape(8, W, W)
    measured = intensities[0, 0]
    info = (where, positions, counts)
    yes = counts[0, 0] >= 0
    shared = [
        vm(4, 256, EC), vm(8, W, W), vm(2, W, W), pltpu.VMEM((2, 3, 2, W, W), bf16), vm(4, 256, EC), vm(9 * W, W),
    ]
    scratch = [
        pltpu.VMEM((12, 2 * W, 2 * W), bf16),
        vm(2, F, W, W),
        pltpu.VMEM((F * W, 6 * W), bf16),
        vm(2, 4, W, W),
        vm(2, F, W, W),
    ]

    me, mo = call(strips_kernel, [sds(2, TR, W)] * 2, (where,), (objects,))
    ce, co = swap(me, mo, COL, 16)
    be, bo = call(widen_kernel, [sds(4, H, EC), sds(4, H, EC)], (where,), (objects, ce, co))
    re, ro = swap(be, bo, ROW, 32)
    e, g, me, mo, keep, give = call(
        first_kernel,
        [sds(4, 256, EC), sds(4, 256, EC), sds(4, 256, W), sds(4, 256, W), sds(HALF, W), sds(HALF, W)],
        info, (objects.reshape(4, TR, TC), ce, co, re, ro, modes, measured, blocks),
        shared + [vm(4, 256, W), vm(4, 256, W), sem(26)] + scratch, cost=ITER_COST, big=True,
    )

    got = other_core(give)
    ce, co = swap(me, mo, COL, 16)
    v = reduce_out(yes, keep, got)
    v, ce, co = lax.optimization_barrier((v, ce, co))
    ge, go = call(
        halves_kernel, [sds(4, TR, EC), sds(4, TR, EC)], (where,), (g, ce, co),
        [vm(4, 256, EC), vm(4, 256, W), vm(4, 256, W), sem(20)], big=True,
    )
    v, ge, go = lax.optimization_barrier((v, ge, go))
    re, ro = swap(ge, go, ROW, 32)
    own = gather_back(yes, v)
    own, re, ro = lax.optimization_barrier((own, re, ro))
    other = other_core(own)
    oc, gc, give, go, keep, modes = call(
        second_kernel,
        [sds(4, TR, TC), sds(4, TR, EC), sds(HALF + 12 * H, W), sds(4, H, EC), sds(HALF, W), sds(8, W, W)],
        info, (e, ge, go, re, ro, modes, own, other, measured, blocks),
        shared + [vm(4, 256, EC), vm(9 * W, W), sem(46)] + scratch, cost=ITER_COST, big=True,
    )

    got = other_core(give)
    ro = odd_swap(go, ROW, 32)
    v = reduce_out(yes, keep, got)
    v, got, ro = lax.optimization_barrier((v, got, ro))
    t, me, mo = call(
        fold_kernel, [sds(4, TR, TC), sds(2, TR, W), sds(2, TR, W)], (where,), (oc, gc, got, ro), [vm(4, TR, EC)],
    )
    v, me, mo = lax.optimization_barrier((v, me, mo))
    ce, co = swap(me, mo, COL, 16)
    own = gather_back(yes, v)
    own, ce, co = lax.optimization_barrier((own, ce, co))
    other = other_core(own)
    (refined,) = call(last_kernel, [sds(2, 2, TR, TC)], (where,), (t, ce, co))
    (modes,) = call(modes_kernel, [sds(8, W, W)], (where,), (modes, own, other), [vm(9 * W, W)])
    return refined, modes.reshape(M, 2, W, W)


def solution(mesh):
    fine = Mesh(mesh.devices.reshape(4, 4, 2, 2, 8), ("x", "yl", "c", "yh", "z"))
    return jax.shard_map(
        body,
        mesh=fine,
        in_specs=(
            P(None, None, ROW, COL),
            P(),
            P(ROW, COL, None, None, None),
            P(ROW, COL, None, None),
            P(ROW, COL),
        ),
        out_specs=(P(None, None, ROW, COL), P()),
        check_vma=False,
    )
```

```python
import math

import jax
import jax.numpy as jnp
import ml_dtypes
import numpy as np
from jax import lax
from jax.experimental import pallas as pl
from jax.experimental.pallas import tpu as pltpu
from jax.sharding import Mesh, PartitionSpec as P

ROW = ("x", "yl", "c")
COL = ("yh", "z")
XZ = ("x", "z")
Y = ("yh", "yl")

W = 128
H = 64
TR = 128
TC = 256
EC = 384
M = 4
WIN = W + 8
F = 8
f32 = jnp.float32
bf16 = jnp.bfloat16


def split_np(a):
    out = []
    for _ in range(3):
        part = a.astype(ml_dtypes.bfloat16)
        out.append(part)
        a = a - part.astype(np.float64)
    return out


def tables_np():
    n = np.arange(W)
    ang = -2.0 * math.pi * ((n[:, None] * n[None, :]) % W) / W
    t = np.exp(1j * ang) / math.sqrt(W)
    f = ((n + H) % W - H).astype(np.float64)
    k = np.exp(-4j * math.pi * f * f / (W * W))
    a = np.conj(t) @ (k[:, None] * t)
    return np.stack([np.stack([np.stack(split_np(m.real)), np.stack(split_np(m.imag))], axis=1) for m in (t, a)])


def lanes(shape):
    return lax.broadcasted_iota(jnp.int32, shape, len(shape) - 1)


def split(x, parts):
    out = []
    for i in range(parts):
        h = x.astype(bf16)
        out.append(h)
        if i < parts - 1:
            x = x - h.astype(f32)
    return out


PAIRS = {2: ((0, 0), (0, 1), (1, 0)), 3: ((0, 0), (0, 1), (1, 0), (0, 2), (1, 1), (2, 0))}


def cmul(ar, ai, br, bi):
    return ar * br - ai * bi, ar * bi + ai * br


def cmulc(ar, ai, br, bi):
    return ar * br + ai * bi, ar * bi - ai * br


def right(z, lhs, tab, i, parts):
    w = jnp.concatenate([tab[i + t] for _, t in PAIRS[parts]], axis=0)
    fs = 256 // W
    for k in range(F // fs):
        rows = slice(k * 256, (k + 1) * 256)
        x = jnp.concatenate([lhs[rows, p * 2 * W : (p + 1) * 2 * W] for p, _ in PAIRS[parts]], axis=1)
        y = jnp.dot(x, w, preferred_element_type=f32)
        z[0, k * fs : (k + 1) * fs] = y[:, :W].reshape(fs, W, W)
        z[1, k * fs : (k + 1) * fs] = y[:, W:].reshape(fs, W, W)


def put_lhs(lhs, f, xr, xi, parts):
    rows = slice(f * W, (f + 1) * W)
    for q, x in enumerate((xr, xi)):
        for p, v in enumerate(split(x, parts)):
            at = (2 * p + q) * W
            lhs[rows, at : at + W] = v


def both(z, lhs, tab, i, parts):
    right(z, lhs, tab, i, parts)
    for f in range(F):
        put_lhs(lhs, f, z[0, f].T, z[1, f].T, parts)
    right(z, lhs, tab, i, parts)


U, UT, B, BT = 0, 3, 6, 9


def build_tables(tab, blocks):
    for j in range(2):
        for part in range(3):
            re = blocks[j, part, 0]
            im = blocks[j, part, 1]
            for i, (ur, ll) in enumerate(((-im, im), (im, -im))):
                k = 6 * j + 3 * i + part
                tab[k, :W, :W] = re
                tab[k, :W, W:] = ur
                tab[k, W:, :W] = ll
                tab[k, W:, W:] = re


def window(r0, s):
    r8 = r0 // 8
    q = s // W
    q1 = jnp.where(q == 2, 0, q + 1)
    rows = pl.ds(pl.multiple_of(r8 * 8, 8), WIN)
    at = [(rows, pl.ds(pl.multiple_of(t * W, W), W)) for t in (q, q1)]
    return at, r0 - r8 * 8, s - q * W


def cut(e, r0, s, plane):
    at, dr, dc = window(r0, s)
    low = lanes((WIN, W)) >= dc
    v = jnp.where(low, e[(plane,) + at[0]], e[(plane,) + at[1]])
    v = pltpu.roll(v, jnp.where(dc == 0, 0, W - dc), 1)
    v = pltpu.roll(v, jnp.where(dr == 0, 0, WIN - dr), 0)
    return v[:W]


def place(g, r0, s, plane, val):
    at, dr, dc = window(r0, s)
    v = jnp.concatenate([val, jnp.zeros((WIN - W, W), f32)], axis=0)
    v = pltpu.roll(v, dr, 0)
    v = pltpu.roll(v, dc, 1)
    low = lanes((WIN, W)) >= dc
    i0 = (plane,) + at[0]
    i1 = (plane,) + at[1]
    g[i0] = g[i0] + jnp.where(low, v, 0.0)
    g[i1] = g[i1] + jnp.where(low, 0.0, v)


def iteration(info, e, p, meas, blocks, g, acc, s, parts, waits):
    tab, z, lhs, o, psi1 = s
    where, positions, counts = info
    rows = [jnp.clip(positions[0, 0, n, 0] - where[0] + H, 0, TR - 1) for n in range(2)]
    cols = [jnp.clip(positions[0, 0, n, 1] - where[1] + W, H, TC + H - 1) for n in range(2)]
    live = [(counts[0, 0] > n).astype(f32) for n in range(2)]
    for k in range(4):
        waits[2](k)
        g[k] = jnp.zeros_like(g[k])
        for n in range(2):
            v = cut(e, rows[n], cols[n], k)
            o[n, k] = v if k < 2 else v.T
    waits[3]()
    wsum = None
    for n in range(2):
        t = (o[n, 0] * o[n, 0] + o[n, 1] * o[n, 1]) * live[n]
        wsum = t if wsum is None else wsum + t
    acc[8 * W :] = wsum
    for f in range(F):
        n, m = divmod(f, M)
        put_lhs(lhs, f, *cmul(p[2 * m], p[2 * m + 1], o[n, 0], o[n, 1]), parts)
    waits[0].wait()
    build_tables(tab, blocks)
    both(psi1, lhs, tab, BT, parts)
    for f in range(F):
        n = f // M
        put_lhs(lhs, f, *cmul(psi1[0, f], psi1[1, f], o[n, 2], o[n, 3]), parts)
    both(z, lhs, tab, UT, parts)
    for n in range(2):
        tot = None
        for f in range(n * M, (n + 1) * M):
            t = z[0, f] * z[0, f] + z[1, f] * z[1, f]
            tot = t if tot is None else tot + t
        if n == 0:
            waits[1].wait()
        wt = 2.0 * (tot - meas[n])
        for f in range(n * M, (n + 1) * M):
            put_lhs(lhs, f, wt * z[0, f], wt * z[1, f], parts)
    both(z, lhs, tab, U, parts)
    for n in range(2):
        sr = si = None
        for f in range(n * M, (n + 1) * M):
            tr, ti = cmulc(psi1[0, f], psi1[1, f], z[0, f], z[1, f])
            sr = tr if sr is None else sr + tr
            si = ti if si is None else si + ti
            put_lhs(lhs, f, *cmulc(o[n, 2], o[n, 3], z[0, f], z[1, f]), parts)
        place(g, rows[n], cols[n], 2, sr.T * live[n])
        place(g, rows[n], cols[n], 3, si.T * live[n])
    waits[4]()
    both(z, lhs, tab, B, parts)
    for n in range(2):
        sr = si = None
        for f in range(n * M, (n + 1) * M):
            m = f - n * M
            tr, ti = cmulc(p[2 * m], p[2 * m + 1], z[0, f], z[1, f])
            sr = tr if sr is None else sr + tr
            si = ti if si is None else si + ti
            for i, v in enumerate(cmulc(o[n, 0], o[n, 1], z[0, f], z[1, f])):
                at = slice((2 * m + i) * W, (2 * m + i + 1) * W)
                acc[at] = v * live[n] if n == 0 else acc[at] + v * live[n]
        place(g, rows[n], cols[n], 0, sr * live[n])
        place(g, rows[n], cols[n], 1, si * live[n])


def start(src, dst, sem):
    c = pltpu.make_async_copy(src, dst, sem)
    c.start()
    return c


def done(copies):
    for c in copies:
        c.wait()


def eight(i):
    return pl.multiple_of(i, 8)


HALF = 576


def send_sums(where, acc, keep, give, sems, i):
    mine = pl.ds(eight(where[2] * HALF), HALF)
    theirs = pl.ds(eight((1 - where[2]) * HALF), HALF)
    return [start(acc.at[mine], keep, sems.at[i]), start(acc.at[theirs], give, sems.at[i + 1])]


def col_messages(where, g, a, b, planes):
    low = lanes((256, W)) < H
    first = where[3] == 0
    for k in planes:
        v = [g[k, :, j * W : (j + 1) * W] for j in range(3)]
        ml = jnp.where(low, v[1], v[0])
        mr = jnp.where(low, v[0], v[2])
        a[k] = jnp.where(first, mr, ml)
        b[k] = jnp.where(first, ml, mr)


def first_kernel(
    where, positions, counts, x, ce, co, ke, ko, even, odd, p_in, meas_in, blocks_in,
    e_out, g_out, me, mo, keep, give,
    e, p, meas, blocks, g, acc, a, b, sems, *s,
):
    up = where[2] == 0
    at = eight(jnp.where(up, H + TR, 0))
    below = eight(H + TR - at)
    strips = [
        start(ce, a.at[0:2, 0:TR, :], sems.at[0]),
        start(co, b.at[0:2, 0:TR, :], sems.at[1]),
        start(ke, a.at[0:2, TR : TR + H, :], sems.at[26]),
        start(ko, b.at[0:2, TR : TR + H, :], sems.at[27]),
    ]
    ins = [
        [
            start(x.at[k], e.at[k, H : H + TR, W:], sems.at[2 + k]),
            start(even.at[k], e.at[k, pl.ds(at, H), :], sems.at[6 + k]),
            start(odd.at[k], e.at[k, pl.ds(below, H), W:], sems.at[10 + k]),
        ]
        for k in range(4)
    ]
    modes_copy = start(p_in, p, sems.at[14])
    tables = start(blocks_in, blocks, sems.at[15])
    measured = start(meas_in, meas, sems.at[16])
    outs = []

    def plane(k):
        if k == 0:
            done(strips)
        done(ins[k])
        first = where[3] == 0
        for src, dst, n in ((slice(0, TR), slice(H, H + TR), TR), (slice(TR, TR + H), pl.ds(below, H), H)):
            va, vb = a[k // 2, src], b[k // 2, src]
            left_in = jnp.where(first, vb, va)
            right_in = jnp.where(first, va, vb)
            e[k, dst, 0:W] = widened(left_in, right_in, k % 2, lanes((n, W)) < H)

    def whole():
        modes_copy.wait()
        outs.append(start(e, e_out, sems.at[17]))

    def ready(planes, i):
        col_messages(where, g, a, b, planes)
        ps = slice(planes[0], planes[-1] + 1)
        outs.append(start(a.at[ps], me.at[ps], sems.at[i]))
        outs.append(start(b.at[ps], mo.at[ps], sems.at[i + 1]))
        outs.append(start(g.at[ps], g_out.at[ps], sems.at[i + 2]))

    iteration(
        (where, positions, counts), e, p, meas, blocks, g, acc, s, 3,
        (tables, measured, plane, whole, lambda: ready((2, 3), 18)),
    )
    outs += send_sums(where, acc, keep, give, sems, 21)
    ready((0, 1), 23)
    done(outs)


def sum_copies(where, own, other, s, sems, i):
    mine = pl.ds(eight(where[2] * HALF), HALF)
    theirs = pl.ds(eight((1 - where[2]) * HALF), HALF)
    return [start(own, s.at[mine], sems.at[i]), start(other, s.at[theirs], sems.at[i + 1])]


def new_modes(p, s):
    inv = 0.25 / jnp.sqrt(s[8 * W :])
    for k in range(8):
        p[k] = p[k] - s[k * W : (k + 1) * W] * inv


def second_kernel(
    where, positions, counts, e_in, ge_in, go_in, even, odd, p_in, own, other, meas_in, blocks_in,
    oc, gc, give, go, keep, p_out,
    e, p, meas, blocks, g, acc, r, sums, sems, *s,
):
    at = eight(jnp.where(where[2] == 0, TR, 0))
    hi = pl.ds(at, TR)
    lo = pl.ds(eight(TR - at), TR)
    ins = [
        [
            start(e_in.at[k], e.at[k], sems.at[5 * k]),
            start(ge_in.at[k], g.at[k, hi, :], sems.at[5 * k + 1]),
            start(go_in.at[k], g.at[k, lo, :], sems.at[5 * k + 2]),
            start(even.at[k], r.at[k, hi, :], sems.at[5 * k + 3]),
            start(odd.at[k], r.at[k, lo, :], sems.at[5 * k + 4]),
        ]
        for k in range(4)
    ]
    sums_copies = [start(p_in, p, sems.at[20])] + sum_copies(where, own, other, sums, sems, 21)
    tables = start(blocks_in, blocks, sems.at[23])
    measured = start(meas_in, meas, sems.at[24])
    outs = []
    up = eight(jnp.where(where[2] == 0, H + TR, 0))
    down = eight(H + TR - up)

    def plane(k):
        done(ins[k])
        e[k] = e[k] - 0.1 * (g[k] + r[k])

    def whole():
        outs.append(start(e.at[:, H : H + TR, W:], oc, sems.at[25]))
        done(sums_copies)
        new_modes(p, sums)
        outs.append(start(p, p_out, sems.at[26]))

    def ready(planes, i):
        ps = slice(planes[0], planes[-1] + 1)
        outs.append(start(g.at[ps, pl.ds(down, H), :], go.at[ps], sems.at[i]))
        outs.append(start(g.at[ps, H : H + TR, :], gc.at[ps], sems.at[i + 1]))
        for k in planes:
            for j in range(3):
                rows = pl.ds(HALF + (3 * k + j) * H, H)
                outs.append(start(g.at[k, pl.ds(up, H), j * W : (j + 1) * W], give.at[rows], sems.at[30 + 3 * k + j]))

    iteration(
        (where, positions, counts), e, p, meas, blocks, g, acc, s, 2,
        (tables, measured, plane, whole, lambda: ready((2, 3), 27)),
    )
    outs += send_sums(where, acc, keep, give.at[pl.ds(0, HALF)], sems, 42)
    ready((0, 1), 44)
    done(outs)


def widened(left_in, right_in, part, low):
    if part == 0:
        return jnp.where(low, right_in, pltpu.roll(left_in, H, 1))
    return jnp.where(low, pltpu.roll(right_in, H, 1), left_in)


def pack(a, b, hi):
    low = lanes(a.shape) < H
    if hi:
        return jnp.where(low, pltpu.roll(a, H, 1), b)
    return jnp.where(low, a, pltpu.roll(b, H, 1))


def strips_kernel(where, x, even, odd, rows_odd, corner_even, corner_odd):
    first = where[3] == 0
    at = pl.ds(eight(jnp.where(where[2] == 0, 0, H)), H)
    for k in range(2):
        ml = pack(x[k, 0, :, 0:W], x[k, 1, :, 0:W], False)
        mr = pack(x[k, 0, :, W:], x[k, 1, :, W:], True)
        even[k] = jnp.where(first, mr, ml)
        odd[k] = jnp.where(first, ml, mr)
        corner_even[k] = even[k, at]
        corner_odd[k] = odd[k, at]
        for j in range(2):
            rows_odd[2 * k + j] = x[k, j, at]


def widen_kernel(where, x, even, odd, out):
    low = lanes((H, W)) < H
    first = where[3] == 0
    rows = pl.ds(eight(jnp.where(where[2] == 0, H, 0)), H)
    for k in range(2):
        left_in = jnp.where(first, odd[k, rows], even[k, rows])
        right_in = jnp.where(first, even[k, rows], odd[k, rows])
        for j in range(2):
            out[2 * k + j, :, 0:W] = widened(left_in, right_in, j, low)
            out[2 * k + j, :, W:] = x[k, j, rows]


def halves_kernel(where, g_in, even, odd, ge, go, g, a, b, sems):
    ins = [
        [
            start(g_in.at[k], g.at[k], sems.at[3 * k]),
            start(even.at[k], a.at[k], sems.at[3 * k + 1]),
            start(odd.at[k], b.at[k], sems.at[3 * k + 2]),
        ]
        for k in range(4)
    ]
    low = lanes((256, W)) < H
    first = where[3] == 0
    at = eight(jnp.where(where[2] == 0, TR, 0))
    outs = []
    for k in range(4):
        done(ins[k])
        rl = jnp.where(first, b[k], a[k])
        rr = jnp.where(first, a[k], b[k])
        g[k, :, 0:W] = g[k, :, 0:W] + jnp.where(low, rr, rl)
        g[k, :, W : 2 * W] = g[k, :, W : 2 * W] + jnp.where(low, rl, 0.0)
        g[k, :, 2 * W :] = g[k, :, 2 * W :] + jnp.where(low, 0.0, rr)
        outs.append(start(g.at[k, pl.ds(at, TR), :], ge.at[k], sems.at[12 + 2 * k]))
        outs.append(start(g.at[k, pl.ds(eight(TR - at), TR), :], go.at[k], sems.at[13 + 2 * k]))
    done(outs)


def fold_kernel(where, oc, gc, even, odd, t, me, mo, r):
    at = eight(jnp.where(where[2] == 0, H, 0))
    for k in range(4):
        for j in range(3):
            r[k, pl.ds(at, H), j * W : (j + 1) * W] = even[HALF + (3 * k + j) * H : HALF + (3 * k + j + 1) * H]
    r[:, pl.ds(eight(H - at), H), :] = odd[...]
    first = where[3] == 0
    for k in range(4):
        t[k] = oc[k] - 0.1 * (gc[k, :, W:] + r[k, :, W:])
    for k in range(2):
        v0 = gc[2 * k, :, 0:W] + r[2 * k, :, 0:W]
        v1 = gc[2 * k + 1, :, 0:W] + r[2 * k + 1, :, 0:W]
        ml = pack(v0, v1, True)
        mr = pack(v0, v1, False)
        me[k] = jnp.where(first, mr, ml)
        mo[k] = jnp.where(first, ml, mr)


def last_kernel(where, t, even, odd, out):
    low = lanes((TR, W)) < H
    first = where[3] == 0
    for k in range(2):
        rl = jnp.where(first, odd[k], even[k])
        rr = jnp.where(first, even[k], odd[k])
        add = (
            (jnp.where(low, rl, 0.0), jnp.where(low, 0.0, pltpu.roll(rr, H, 1))),
            (jnp.where(low, pltpu.roll(rl, H, 1), 0.0), jnp.where(low, 0.0, rr)),
        )
        for j in range(2):
            for h in range(2):
                cs = slice(h * W, (h + 1) * W)
                out[k, j, :, cs] = t[2 * k + j, :, cs] - 0.1 * add[j][h]


def modes_kernel(where, p, own, other, out, s):
    s[pl.ds(eight(where[2] * HALF), HALF)] = own[...]
    s[pl.ds(eight((1 - where[2]) * HALF), HALF)] = other[...]
    out[...] = p[...]
    new_modes(out, s)


HB = pl.BlockSpec(memory_space=pltpu.HBM)
VM = pl.BlockSpec(memory_space=pltpu.VMEM)
SM = pl.BlockSpec(memory_space=pltpu.SMEM)


def sds(*shape):
    return jax.ShapeDtypeStruct(shape, f32)


def vm(*shape):
    return pltpu.VMEM(shape, f32)


def sem(n):
    return pltpu.SemaphoreType.DMA((n,))


def call(kernel, outs, smem, args, scratch=(), cost=None, big=False):
    spec = HB if big else VM
    return pl.pallas_call(
        kernel,
        out_shape=outs,
        in_specs=[SM] * len(smem) + [spec] * len(args),
        out_specs=[spec] * len(outs),
        scratch_shapes=list(scratch),
        compiler_params=pltpu.CompilerParams(vmem_limit_bytes=(52 if big else 12) * 1024 * 1024),
        cost_estimate=cost,
    )(*smem, *args)


def even_partner(i):
    return i ^ 1


def odd_partner(i):
    return ((i + 1) ^ 1) - 1


def odd_swap(odd, axes, size):
    return lax.ppermute(odd, axes, [(i, odd_partner(i)) for i in range(1, size - 1)])


def swap(even, odd, axes, size):
    return lax.ppermute(even, axes, [(i, even_partner(i)) for i in range(size)]), odd_swap(odd, axes, size)


def corner_swap(v, partner, skip):
    pairs = [
        (16 * i + j, 16 * odd_partner(i) + partner(j)) for i in range(1, 31) for j in range(skip, 16 - skip)
    ]
    return lax.ppermute(v, ROW + COL, pairs)


def other_core(v):
    return lax.ppermute(v, "c", [(0, 1), (1, 0)])


def scatter_sum(v, axes, n):
    v = lax.all_to_all(v.reshape(n, 1, -1), axes, 0, 0, tiled=True)
    return jnp.sum(v, axis=(0, 1))


def spread(v, axes, n):
    w = jnp.broadcast_to(v[None, None], (n, 1) + v.shape)
    return lax.all_to_all(w, axes, 0, 0, tiled=True)


def apart(yes, f, shape):
    return lax.cond(yes, f, lambda: jnp.zeros(shape, f32))


def reduce_out(yes, keep, got):
    def step():
        v = scatter_sum(keep + got[:HALF], XZ, 32)
        return jnp.sum(spread(v, Y, 8), axis=(0, 1))

    return apart(yes, step, (2304,))


def gather_back(yes, v):
    return apart(yes, lambda: spread(v, XZ, 32).reshape(HALF, W), (HALF, W))


ITER_COST = pl.CostEstimate(flops=10_000_000_000, bytes_accessed=8_000_000, transcendentals=0)


def body(objects, probe_modes, intensities, positions, counts):
    blocks = jnp.asarray(tables_np())
    where = jnp.stack([
        lax.axis_index(ROW) * TR,
        lax.axis_index(COL) * TC,
        lax.axis_index("c"),
        lax.axis_index("z") % 2,
    ]).astype(jnp.int32)
    modes = probe_modes.reshape(8, W, W)
    measured = intensities[0, 0]
    info = (where, positions, counts)
    yes = counts[0, 0] >= 0
    shared = [
        vm(4, 256, EC), vm(8, W, W), vm(2, W, W), pltpu.VMEM((2, 3, 2, W, W), bf16), vm(4, 256, EC), vm(9 * W, W),
    ]
    scratch = [
        pltpu.VMEM((12, 2 * W, 2 * W), bf16),
        vm(2, F, W, W),
        pltpu.VMEM((F * W, 6 * W), bf16),
        vm(2, 4, W, W),
        vm(2, F, W, W),
    ]

    me, mo, rows_odd, ke, ko = call(
        strips_kernel, [sds(2, TR, W)] * 2 + [sds(4, H, TC)] + [sds(2, H, W)] * 2, (where,), (objects,)
    )
    ce, co = swap(me, mo, COL, 16)
    ro = odd_swap(rows_odd, ROW, 32)
    ke = corner_swap(ke, even_partner, 0)
    ko = corner_swap(ko, odd_partner, 1)
    ce, co, ro, ke, ko = lax.optimization_barrier((ce, co, ro, ke, ko))
    (be,) = call(widen_kernel, [sds(4, H, EC)], (where,), (objects, ce, co))
    re = lax.ppermute(be, ROW, [(i, even_partner(i)) for i in range(32)])
    e, g, me, mo, keep, give = call(
        first_kernel,
        [sds(4, 256, EC), sds(4, 256, EC), sds(4, 256, W), sds(4, 256, W), sds(HALF, W), sds(HALF, W)],
        info, (objects.reshape(4, TR, TC), ce, co, ke, ko, re, ro, modes, measured, blocks),
        shared + [vm(4, 256, W), vm(4, 256, W), sem(28)] + scratch, cost=ITER_COST, big=True,
    )

    got = other_core(give)
    ce, co = swap(me, mo, COL, 16)
    v = reduce_out(yes, keep, got)
    v, ce, co = lax.optimization_barrier((v, ce, co))
    ge, go = call(
        halves_kernel, [sds(4, TR, EC), sds(4, TR, EC)], (where,), (g, ce, co),
        [vm(4, 256, EC), vm(4, 256, W), vm(4, 256, W), sem(20)], big=True,
    )
    v, ge, go = lax.optimization_barrier((v, ge, go))
    re, ro = swap(ge, go, ROW, 32)
    own = gather_back(yes, v)
    own, re, ro = lax.optimization_barrier((own, re, ro))
    other = other_core(own)
    oc, gc, give, go, keep, modes = call(
        second_kernel,
        [sds(4, TR, TC), sds(4, TR, EC), sds(HALF + 12 * H, W), sds(4, H, EC), sds(HALF, W), sds(8, W, W)],
        info, (e, ge, go, re, ro, modes, own, other, measured, blocks),
        shared + [vm(4, 256, EC), vm(9 * W, W), sem(46)] + scratch, cost=ITER_COST, big=True,
    )

    got = other_core(give)
    ro = odd_swap(go, ROW, 32)
    v = reduce_out(yes, keep, got)
    v, got, ro = lax.optimization_barrier((v, got, ro))
    t, me, mo = call(
        fold_kernel, [sds(4, TR, TC), sds(2, TR, W), sds(2, TR, W)], (where,), (oc, gc, got, ro), [vm(4, TR, EC)],
    )
    v, me, mo = lax.optimization_barrier((v, me, mo))
    ce, co = swap(me, mo, COL, 16)
    own = gather_back(yes, v)
    own, ce, co = lax.optimization_barrier((own, ce, co))
    other = other_core(own)
    (refined,) = call(last_kernel, [sds(2, 2, TR, TC)], (where,), (t, ce, co))
    (modes,) = call(modes_kernel, [sds(8, W, W)], (where,), (modes, own, other), [vm(9 * W, W)])
    return refined, modes.reshape(M, 2, W, W)


def solution(mesh):
    fine = Mesh(mesh.devices.reshape(4, 4, 2, 2, 8), ("x", "yl", "c", "yh", "z"))
    return jax.shard_map(
        body,
        mesh=fine,
        in_specs=(
            P(None, None, ROW, COL),
            P(),
            P(ROW, COL, None, None, None),
            P(ROW, COL, None, None),
            P(ROW, COL),
        ),
        out_specs=(P(None, None, ROW, COL), P()),
        check_vma=False,
    )
```

```python
import math

import jax
import jax.numpy as jnp
import ml_dtypes
import numpy as np
from jax import lax
from jax.experimental import pallas as pl
from jax.experimental.pallas import tpu as pltpu
from jax.sharding import Mesh, PartitionSpec as P

ROW = ("x", "yl", "c")
COL = ("yh", "z")
XZ = ("x", "z")
Y = ("yh", "yl")

W = 128
H = 64
TR = 128
TC = 256
EC = 384
M = 4
WIN = W + 8
F = 8
f32 = jnp.float32
bf16 = jnp.bfloat16


def split_np(a):
    out = []
    for _ in range(3):
        part = a.astype(ml_dtypes.bfloat16)
        out.append(part)
        a = a - part.astype(np.float64)
    return out


def tables_np():
    n = np.arange(W)
    ang = -2.0 * math.pi * ((n[:, None] * n[None, :]) % W) / W
    t = np.exp(1j * ang) / math.sqrt(W)
    f = ((n + H) % W - H).astype(np.float64)
    k = np.exp(-4j * math.pi * f * f / (W * W))
    a = np.conj(t) @ (k[:, None] * t)
    return np.stack([np.stack([np.stack(split_np(m.real)), np.stack(split_np(m.imag))], axis=1) for m in (t, a)])


def lanes(shape):
    return lax.broadcasted_iota(jnp.int32, shape, len(shape) - 1)


def split(x, parts):
    out = []
    for i in range(parts):
        h = x.astype(bf16)
        out.append(h)
        if i < parts - 1:
            x = x - h.astype(f32)
    return out


PAIRS = {2: ((0, 0), (0, 1), (1, 0)), 3: ((0, 0), (0, 1), (1, 0), (0, 2), (1, 1), (2, 0))}


def cmul(ar, ai, br, bi):
    return ar * br - ai * bi, ar * bi + ai * br


def cmulc(ar, ai, br, bi):
    return ar * br + ai * bi, ar * bi - ai * br


def right(z, lhs, tab, i, parts):
    w = jnp.concatenate([tab[i + t] for _, t in PAIRS[parts]], axis=0)
    fs = 256 // W
    for k in range(F // fs):
        rows = slice(k * 256, (k + 1) * 256)
        x = jnp.concatenate([lhs[rows, p * 2 * W : (p + 1) * 2 * W] for p, _ in PAIRS[parts]], axis=1)
        y = jnp.dot(x, w, preferred_element_type=f32)
        z[0, k * fs : (k + 1) * fs] = y[:, :W].reshape(fs, W, W)
        z[1, k * fs : (k + 1) * fs] = y[:, W:].reshape(fs, W, W)


def put_lhs(lhs, f, xr, xi, parts):
    rows = slice(f * W, (f + 1) * W)
    for q, x in enumerate((xr, xi)):
        for p, v in enumerate(split(x, parts)):
            at = (2 * p + q) * W
            lhs[rows, at : at + W] = v


def both(z, lhs, tab, i, parts):
    right(z, lhs, tab, i, parts)
    for f in range(F):
        put_lhs(lhs, f, z[0, f].T, z[1, f].T, parts)
    right(z, lhs, tab, i, parts)


U, UT, B, BT = 0, 3, 6, 9


def build_tables(tab, blocks):
    for j in range(2):
        for part in range(3):
            re = blocks[j, part, 0]
            im = blocks[j, part, 1]
            for i, (ur, ll) in enumerate(((-im, im), (im, -im))):
                k = 6 * j + 3 * i + part
                tab[k, :W, :W] = re
                tab[k, :W, W:] = ur
                tab[k, W:, :W] = ll
                tab[k, W:, W:] = re


def window(r0, s):
    r8 = r0 // 8
    q = s // W
    q1 = jnp.where(q == 2, 0, q + 1)
    rows = pl.ds(pl.multiple_of(r8 * 8, 8), WIN)
    at = [(rows, pl.ds(pl.multiple_of(t * W, W), W)) for t in (q, q1)]
    return at, r0 - r8 * 8, s - q * W


def cut(e, r0, s, plane):
    at, dr, dc = window(r0, s)
    low = lanes((WIN, W)) >= dc
    v = jnp.where(low, e[(plane,) + at[0]], e[(plane,) + at[1]])
    v = pltpu.roll(v, jnp.where(dc == 0, 0, W - dc), 1)
    v = pltpu.roll(v, jnp.where(dr == 0, 0, WIN - dr), 0)
    return v[:W]


def place(g, r0, s, plane, val):
    at, dr, dc = window(r0, s)
    v = jnp.concatenate([val, jnp.zeros((WIN - W, W), f32)], axis=0)
    v = pltpu.roll(v, dr, 0)
    v = pltpu.roll(v, dc, 1)
    low = lanes((WIN, W)) >= dc
    i0 = (plane,) + at[0]
    i1 = (plane,) + at[1]
    g[i0] = g[i0] + jnp.where(low, v, 0.0)
    g[i1] = g[i1] + jnp.where(low, 0.0, v)


def iteration(info, e, p, meas, blocks, g, acc, s, parts, waits):
    tab, z, lhs, o, psi1 = s
    where, positions, counts = info
    rows = [jnp.clip(positions[0, 0, n, 0] - where[0] + H, 0, TR - 1) for n in range(2)]
    cols = [jnp.clip(positions[0, 0, n, 1] - where[1] + W, H, TC + H - 1) for n in range(2)]
    live = [(counts[0, 0] > n).astype(f32) for n in range(2)]
    for k in range(4):
        waits[2](k)
        g[k] = jnp.zeros_like(g[k])
        for n in range(2):
            v = cut(e, rows[n], cols[n], k)
            o[n, k] = v if k < 2 else v.T
    waits[3]()
    wsum = None
    for n in range(2):
        t = (o[n, 0] * o[n, 0] + o[n, 1] * o[n, 1]) * live[n]
        wsum = t if wsum is None else wsum + t
    acc[8 * W :] = wsum
    for f in range(F):
        n, m = divmod(f, M)
        put_lhs(lhs, f, *cmul(p[2 * m], p[2 * m + 1], o[n, 0], o[n, 1]), parts)
    waits[0].wait()
    build_tables(tab, blocks)
    both(psi1, lhs, tab, BT, parts)
    for f in range(F):
        n = f // M
        put_lhs(lhs, f, *cmul(psi1[0, f], psi1[1, f], o[n, 2], o[n, 3]), parts)
    both(z, lhs, tab, UT, parts)
    for n in range(2):
        tot = None
        for f in range(n * M, (n + 1) * M):
            t = z[0, f] * z[0, f] + z[1, f] * z[1, f]
            tot = t if tot is None else tot + t
        if n == 0:
            waits[1].wait()
        wt = 2.0 * (tot - meas[n])
        for f in range(n * M, (n + 1) * M):
            put_lhs(lhs, f, wt * z[0, f], wt * z[1, f], parts)
    both(z, lhs, tab, U, parts)
    for n in range(2):
        sr = si = None
        for f in range(n * M, (n + 1) * M):
            tr, ti = cmulc(psi1[0, f], psi1[1, f], z[0, f], z[1, f])
            sr = tr if sr is None else sr + tr
            si = ti if si is None else si + ti
            put_lhs(lhs, f, *cmulc(o[n, 2], o[n, 3], z[0, f], z[1, f]), parts)
        place(g, rows[n], cols[n], 2, sr.T * live[n])
        place(g, rows[n], cols[n], 3, si.T * live[n])
    waits[4]()
    both(z, lhs, tab, B, parts)
    for n in range(2):
        sr = si = None
        for f in range(n * M, (n + 1) * M):
            m = f - n * M
            tr, ti = cmulc(p[2 * m], p[2 * m + 1], z[0, f], z[1, f])
            sr = tr if sr is None else sr + tr
            si = ti if si is None else si + ti
            for i, v in enumerate(cmulc(o[n, 0], o[n, 1], z[0, f], z[1, f])):
                at = slice((2 * m + i) * W, (2 * m + i + 1) * W)
                acc[at] = v * live[n] if n == 0 else acc[at] + v * live[n]
        place(g, rows[n], cols[n], 0, sr * live[n])
        place(g, rows[n], cols[n], 1, si * live[n])


def start(src, dst, sem):
    c = pltpu.make_async_copy(src, dst, sem)
    c.start()
    return c


def done(copies):
    for c in copies:
        c.wait()


def eight(i):
    return pl.multiple_of(i, 8)


HALF = 576


def send_sums(where, acc, keep, give, sems, i):
    mine = pl.ds(eight(where[2] * HALF), HALF)
    theirs = pl.ds(eight((1 - where[2]) * HALF), HALF)
    return [start(acc.at[mine], keep, sems.at[i]), start(acc.at[theirs], give, sems.at[i + 1])]


def col_messages(where, g, a, b, planes):
    low = lanes((256, W)) < H
    first = where[3] == 0
    for k in planes:
        v = [g[k, :, j * W : (j + 1) * W] for j in range(3)]
        ml = jnp.where(low, v[1], v[0])
        mr = jnp.where(low, v[0], v[2])
        a[k] = jnp.where(first, mr, ml)
        b[k] = jnp.where(first, ml, mr)


def first_kernel(
    where, positions, counts, x, ce, co, ke, ko, even, odd, p_in, meas_in, blocks_in,
    e_out, g_out, me, mo, keep, give,
    e, p, meas, blocks, g, acc, a, b, sems, *s,
):
    up = where[2] == 0
    at = eight(jnp.where(up, H + TR, 0))
    below = eight(H + TR - at)
    strips = [
        start(ce, a.at[0:2, 0:TR, :], sems.at[0]),
        start(co, b.at[0:2, 0:TR, :], sems.at[1]),
        start(ke, a.at[0:2, TR : TR + H, :], sems.at[26]),
        start(ko, b.at[0:2, TR : TR + H, :], sems.at[27]),
    ]
    ins = [
        [
            start(x.at[k], e.at[k, H : H + TR, W:], sems.at[2 + k]),
            start(even.at[k], e.at[k, pl.ds(at, H), :], sems.at[6 + k]),
            start(odd.at[k], e.at[k, pl.ds(below, H), W:], sems.at[10 + k]),
        ]
        for k in range(4)
    ]
    modes_copy = start(p_in, p, sems.at[14])
    tables = start(blocks_in, blocks, sems.at[15])
    measured = start(meas_in, meas, sems.at[16])
    outs = []

    def plane(k):
        if k == 0:
            done(strips)
        done(ins[k])
        first = where[3] == 0
        for src, dst, n in ((slice(0, TR), slice(H, H + TR), TR), (slice(TR, TR + H), pl.ds(below, H), H)):
            va, vb = a[k // 2, src], b[k // 2, src]
            left_in = jnp.where(first, vb, va)
            right_in = jnp.where(first, va, vb)
            e[k, dst, 0:W] = widened(left_in, right_in, k % 2, lanes((n, W)) < H)

    def whole():
        modes_copy.wait()
        outs.append(start(e, e_out, sems.at[17]))

    def ready(planes, i):
        col_messages(where, g, a, b, planes)
        ps = slice(planes[0], planes[-1] + 1)
        outs.append(start(a.at[ps], me.at[ps], sems.at[i]))
        outs.append(start(b.at[ps], mo.at[ps], sems.at[i + 1]))
        outs.append(start(g.at[ps], g_out.at[ps], sems.at[i + 2]))

    iteration(
        (where, positions, counts), e, p, meas, blocks, g, acc, s, 3,
        (tables, measured, plane, whole, lambda: ready((2, 3), 18)),
    )
    outs += send_sums(where, acc, keep, give, sems, 21)
    ready((0, 1), 23)
    done(outs)


def sum_copies(where, own, other, s, sems, i):
    mine = pl.ds(eight(where[2] * HALF), HALF)
    theirs = pl.ds(eight((1 - where[2]) * HALF), HALF)
    return [start(own, s.at[mine], sems.at[i]), start(other, s.at[theirs], sems.at[i + 1])]


def new_modes(p, s):
    inv = 0.25 / jnp.sqrt(s[8 * W :])
    for k in range(8):
        p[k] = p[k] - s[k * W : (k + 1) * W] * inv


def second_kernel(
    where, positions, counts, e_in, ge_in, go_in, even, odd, p_in, own, other, meas_in, blocks_in,
    oc, gc, give, go, keep, p_out,
    e, p, meas, blocks, g, acc, r, sums, sems, *s,
):
    at = eight(jnp.where(where[2] == 0, TR, 0))
    hi = pl.ds(at, TR)
    lo = pl.ds(eight(TR - at), TR)
    ins = [
        [
            start(e_in.at[k], e.at[k], sems.at[5 * k]),
            start(ge_in.at[k], g.at[k, hi, :], sems.at[5 * k + 1]),
            start(go_in.at[k], g.at[k, lo, :], sems.at[5 * k + 2]),
            start(even.at[k], r.at[k, hi, :], sems.at[5 * k + 3]),
            start(odd.at[k], r.at[k, lo, :], sems.at[5 * k + 4]),
        ]
        for k in range(4)
    ]
    sums_copies = [start(p_in, p, sems.at[20])] + sum_copies(where, own, other, sums, sems, 21)
    tables = start(blocks_in, blocks, sems.at[23])
    measured = start(meas_in, meas, sems.at[24])
    outs = []
    up = eight(jnp.where(where[2] == 0, H + TR, 0))
    down = eight(H + TR - up)

    def plane(k):
        done(ins[k])
        e[k] = e[k] - 0.1 * (g[k] + r[k])

    def whole():
        outs.append(start(e.at[:, H : H + TR, W:], oc, sems.at[25]))
        done(sums_copies)
        new_modes(p, sums)
        outs.append(start(p, p_out, sems.at[26]))

    def ready(planes, i):
        ps = slice(planes[0], planes[-1] + 1)
        outs.append(start(g.at[ps, pl.ds(down, H), :], go.at[ps], sems.at[i]))
        outs.append(start(g.at[ps, H : H + TR, :], gc.at[ps], sems.at[i + 1]))
        for k in planes:
            for j in range(3):
                rows = pl.ds(HALF + (3 * k + j) * H, H)
                outs.append(start(g.at[k, pl.ds(up, H), j * W : (j + 1) * W], give.at[rows], sems.at[30 + 3 * k + j]))

    iteration(
        (where, positions, counts), e, p, meas, blocks, g, acc, s, 2,
        (tables, measured, plane, whole, lambda: ready((2, 3), 27)),
    )
    outs += send_sums(where, acc, keep, give.at[pl.ds(0, HALF)], sems, 42)
    ready((0, 1), 44)
    done(outs)


def widened(left_in, right_in, part, low):
    if part == 0:
        return jnp.where(low, right_in, pltpu.roll(left_in, H, 1))
    return jnp.where(low, pltpu.roll(right_in, H, 1), left_in)


def pack(a, b, hi):
    low = lanes(a.shape) < H
    if hi:
        return jnp.where(low, pltpu.roll(a, H, 1), b)
    return jnp.where(low, a, pltpu.roll(b, H, 1))


def strips_kernel(where, x, even, odd, rows_odd, corner_even, corner_odd):
    first = where[3] == 0
    at = pl.ds(eight(jnp.where(where[2] == 0, 0, H)), H)
    for k in range(2):
        ml = pack(x[k, 0, :, 0:W], x[k, 1, :, 0:W], False)
        mr = pack(x[k, 0, :, W:], x[k, 1, :, W:], True)
        even[k] = jnp.where(first, mr, ml)
        odd[k] = jnp.where(first, ml, mr)
        corner_even[k] = even[k, at]
        corner_odd[k] = odd[k, at]
        for j in range(2):
            rows_odd[2 * k + j] = x[k, j, at]


def widen_kernel(where, x, even, odd, out):
    low = lanes((H, W)) < H
    first = where[3] == 0
    rows = pl.ds(eight(jnp.where(where[2] == 0, H, 0)), H)
    for k in range(2):
        left_in = jnp.where(first, odd[k, rows], even[k, rows])
        right_in = jnp.where(first, even[k, rows], odd[k, rows])
        for j in range(2):
            out[2 * k + j, :, 0:W] = widened(left_in, right_in, j, low)
            out[2 * k + j, :, W:] = x[k, j, rows]


def halves_kernel(where, g, even, odd, ge, go):
    low = lanes((TR, W)) < H
    first = where[3] == 0
    at = eight(jnp.where(where[2] == 0, TR, 0))
    for out, rows in ((ge, pl.ds(at, TR)), (go, pl.ds(eight(TR - at), TR))):
        for k in range(4):
            rl = jnp.where(first, odd[k, rows], even[k, rows])
            rr = jnp.where(first, even[k, rows], odd[k, rows])
            out[k, :, 0:W] = g[k, rows, 0:W] + jnp.where(low, rr, rl)
            out[k, :, W : 2 * W] = g[k, rows, W : 2 * W] + jnp.where(low, rl, 0.0)
            out[k, :, 2 * W :] = g[k, rows, 2 * W :] + jnp.where(low, 0.0, rr)


def fold_kernel(where, oc, gc, even, odd, t, me, mo, r):
    at = eight(jnp.where(where[2] == 0, H, 0))
    for k in range(4):
        for j in range(3):
            r[k, pl.ds(at, H), j * W : (j + 1) * W] = even[HALF + (3 * k + j) * H : HALF + (3 * k + j + 1) * H]
    r[:, pl.ds(eight(H - at), H), :] = odd[...]
    first = where[3] == 0
    for k in range(4):
        t[k] = oc[k] - 0.1 * (gc[k, :, W:] + r[k, :, W:])
    for k in range(2):
        v0 = gc[2 * k, :, 0:W] + r[2 * k, :, 0:W]
        v1 = gc[2 * k + 1, :, 0:W] + r[2 * k + 1, :, 0:W]
        ml = pack(v0, v1, True)
        mr = pack(v0, v1, False)
        me[k] = jnp.where(first, mr, ml)
        mo[k] = jnp.where(first, ml, mr)


def last_kernel(where, t, even, odd, out):
    low = lanes((TR, W)) < H
    first = where[3] == 0
    for k in range(2):
        rl = jnp.where(first, odd[k], even[k])
        rr = jnp.where(first, even[k], odd[k])
        add = (
            (jnp.where(low, rl, 0.0), jnp.where(low, 0.0, pltpu.roll(rr, H, 1))),
            (jnp.where(low, pltpu.roll(rl, H, 1), 0.0), jnp.where(low, 0.0, rr)),
        )
        for j in range(2):
            for h in range(2):
                cs = slice(h * W, (h + 1) * W)
                out[k, j, :, cs] = t[2 * k + j, :, cs] - 0.1 * add[j][h]


def modes_kernel(where, p, own, other, out, s):
    s[pl.ds(eight(where[2] * HALF), HALF)] = own[...]
    s[pl.ds(eight((1 - where[2]) * HALF), HALF)] = other[...]
    out[...] = p[...]
    new_modes(out, s)


HB = pl.BlockSpec(memory_space=pltpu.HBM)
VM = pl.BlockSpec(memory_space=pltpu.VMEM)
SM = pl.BlockSpec(memory_space=pltpu.SMEM)


def sds(*shape):
    return jax.ShapeDtypeStruct(shape, f32)


def vm(*shape):
    return pltpu.VMEM(shape, f32)


def sem(n):
    return pltpu.SemaphoreType.DMA((n,))


def call(kernel, outs, smem, args, scratch=(), cost=None, big=False):
    spec = HB if big else VM
    return pl.pallas_call(
        kernel,
        out_shape=outs,
        in_specs=[SM] * len(smem) + [spec] * len(args),
        out_specs=[spec] * len(outs),
        scratch_shapes=list(scratch),
        compiler_params=pltpu.CompilerParams(vmem_limit_bytes=(52 if big else 12) * 1024 * 1024),
        cost_estimate=cost,
    )(*smem, *args)


def even_partner(i):
    return i ^ 1


def odd_partner(i):
    return ((i + 1) ^ 1) - 1


def odd_swap(odd, axes, size):
    return lax.ppermute(odd, axes, [(i, odd_partner(i)) for i in range(1, size - 1)])


def swap(even, odd, axes, size):
    return lax.ppermute(even, axes, [(i, even_partner(i)) for i in range(size)]), odd_swap(odd, axes, size)


def corner_swap(v, partner, skip):
    pairs = [
        (16 * i + j, 16 * odd_partner(i) + partner(j)) for i in range(1, 31) for j in range(skip, 16 - skip)
    ]
    return lax.ppermute(v, ROW + COL, pairs)


def other_core(v):
    return lax.ppermute(v, "c", [(0, 1), (1, 0)])


def scatter_sum(v, axes, n):
    v = lax.all_to_all(v.reshape(n, 1, -1), axes, 0, 0, tiled=True)
    return jnp.sum(v, axis=(0, 1))


def spread(v, axes, n):
    w = jnp.broadcast_to(v[None, None], (n, 1) + v.shape)
    return lax.all_to_all(w, axes, 0, 0, tiled=True)


def apart(yes, f, shape):
    return lax.cond(yes, f, lambda: jnp.zeros(shape, f32))


def reduce_out(yes, keep, got):
    def step():
        v = scatter_sum(keep + got[:HALF], XZ, 32)
        return jnp.sum(spread(v, Y, 8), axis=(0, 1))

    return apart(yes, step, (2304,))


def gather_back(yes, v):
    return apart(yes, lambda: spread(v, XZ, 32).reshape(HALF, W), (HALF, W))


ITER_COST = pl.CostEstimate(flops=10_000_000_000, bytes_accessed=8_000_000, transcendentals=0)


def body(objects, probe_modes, intensities, positions, counts):
    blocks = jnp.asarray(tables_np())
    where = jnp.stack([
        lax.axis_index(ROW) * TR,
        lax.axis_index(COL) * TC,
        lax.axis_index("c"),
        lax.axis_index("z") % 2,
    ]).astype(jnp.int32)
    modes = probe_modes.reshape(8, W, W)
    measured = intensities[0, 0]
    info = (where, positions, counts)
    yes = counts[0, 0] >= 0
    shared = [
        vm(4, 256, EC), vm(8, W, W), vm(2, W, W), pltpu.VMEM((2, 3, 2, W, W), bf16), vm(4, 256, EC), vm(9 * W, W),
    ]
    scratch = [
        pltpu.VMEM((12, 2 * W, 2 * W), bf16),
        vm(2, F, W, W),
        pltpu.VMEM((F * W, 6 * W), bf16),
        vm(2, 4, W, W),
        vm(2, F, W, W),
    ]

    me, mo, rows_odd, ke, ko = call(
        strips_kernel, [sds(2, TR, W)] * 2 + [sds(4, H, TC)] + [sds(2, H, W)] * 2, (where,), (objects,)
    )
    ce, co = swap(me, mo, COL, 16)
    ro = odd_swap(rows_odd, ROW, 32)
    ke = corner_swap(ke, even_partner, 0)
    ko = corner_swap(ko, odd_partner, 1)
    ce, co, ro, ke, ko = lax.optimization_barrier((ce, co, ro, ke, ko))
    (be,) = call(widen_kernel, [sds(4, H, EC)], (where,), (objects, ce, co))
    re = lax.ppermute(be, ROW, [(i, even_partner(i)) for i in range(32)])
    e, g, me, mo, keep, give = call(
        first_kernel,
        [sds(4, 256, EC), sds(4, 256, EC), sds(4, 256, W), sds(4, 256, W), sds(HALF, W), sds(HALF, W)],
        info, (objects.reshape(4, TR, TC), ce, co, ke, ko, re, ro, modes, measured, blocks),
        shared + [vm(4, 256, W), vm(4, 256, W), sem(28)] + scratch, cost=ITER_COST, big=True,
    )

    got = other_core(give)
    ce, co = swap(me, mo, COL, 16)
    v = reduce_out(yes, keep, got)
    v, ce, co = lax.optimization_barrier((v, ce, co))
    ge, go = call(halves_kernel, [sds(4, TR, EC), sds(4, TR, EC)], (where,), (g, ce, co))
    v, ge, go = lax.optimization_barrier((v, ge, go))
    re, ro = swap(ge, go, ROW, 32)
    own = gather_back(yes, v)
    own, re, ro = lax.optimization_barrier((own, re, ro))
    other = other_core(own)
    oc, gc, give, go, keep, modes = call(
        second_kernel,
        [sds(4, TR, TC), sds(4, TR, EC), sds(HALF + 12 * H, W), sds(4, H, EC), sds(HALF, W), sds(8, W, W)],
        info, (e, ge, go, re, ro, modes, own, other, measured, blocks),
        shared + [vm(4, 256, EC), vm(9 * W, W), sem(46)] + scratch, cost=ITER_COST, big=True,
    )

    got = other_core(give)
    ro = odd_swap(go, ROW, 32)
    v = reduce_out(yes, keep, got)
    v, got, ro = lax.optimization_barrier((v, got, ro))
    t, me, mo = call(
        fold_kernel, [sds(4, TR, TC), sds(2, TR, W), sds(2, TR, W)], (where,), (oc, gc, got, ro), [vm(4, TR, EC)],
    )
    v, me, mo = lax.optimization_barrier((v, me, mo))
    ce, co = swap(me, mo, COL, 16)
    own = gather_back(yes, v)
    own, ce, co = lax.optimization_barrier((own, ce, co))
    other = other_core(own)
    (refined,) = call(last_kernel, [sds(2, 2, TR, TC)], (where,), (t, ce, co))
    (modes,) = call(modes_kernel, [sds(8, W, W)], (where,), (modes, own, other), [vm(9 * W, W)])
    return refined, modes.reshape(M, 2, W, W)


def solution(mesh):
    fine = Mesh(mesh.devices.reshape(4, 4, 2, 2, 8), ("x", "yl", "c", "yh", "z"))
    return jax.shard_map(
        body,
        mesh=fine,
        in_specs=(
            P(None, None, ROW, COL),
            P(),
            P(ROW, COL, None, None, None),
            P(ROW, COL, None, None),
            P(ROW, COL),
        ),
        out_specs=(P(None, None, ROW, COL), P()),
        check_vma=False,
    )
```
